32 devices in a mesh: parts: 2 (over y), att: 4 (over x, core), ffn: 4 (over z).
Axes of the slice: x: 2, y: 2, z: 4, core: 2. Of those that a mesh axis runs over, the one named last changes fastest.
Arguments:
- incoming: bfloat16 [128, 2, 8192], P('parts', None, 'att'), parts along dimension 0, may hold values from -60 to 60
- queries: bfloat16 [128, 2, 8192], P(('parts', 'att'), None, 'ffn'), parts along dimension 0, may hold values from -19 to 19
- new_kv: bfloat16 [128, 2, 2048], P(('parts', 'att'), None, 'ffn'), parts along dimension 0, may hold values from -6 to 6
- cache: bfloat16 [128, 640, 2048], P(('parts', 'att'), None, 'ffn'), parts along dimension 0, may hold values from -6 to 6
- lengths: int32 [128], P(('parts', 'att')), parts along dimension 0, may hold values from 1 to 640, 20480 in all
- slot_of: int32 [128], P('parts'), parts along dimension 0, may hold values from 0 to 63, each once
- w_out: bfloat16 [8192, 8192], P('ffn', 'att'), may hold values from -0.0625 to 0.0625
- norm_gain: float32 [8192], P('att'), may hold values from 0.5 to 1.5
- w_gate: bfloat16 [8192, 14336], P('att', 'ffn'), may hold values from -0.0625 to 0.0625
- w_up: bfloat16 [8192, 14336], P('att', 'ffn'), may hold values from -0.0625 to 0.0625
- w_down: bfloat16 [14336, 8192], P('ffn', 'att'), may hold values from -0.046875 to 0.046875
Outputs:
- out: bfloat16 [128, 2, 8192], P(('parts', 'ffn'), None, 'att'), parts along dimension 0
The draws below stay inside these ranges and needn't reach their ends.
There are 2 independent parts, one for each index of `parts`. The reference program is written for one: setup_inputs(seed, part) draws one part's arguments, and reference() takes and returns one part's arrays. A program takes and returns all parts, laid end to end along the dimension named above; an argument that names none is the same for every part. Nothing has to cross between parts.
Inputs may be any that keep to these rules, and one draw needn't show every extreme that they name: In each part, the kept lengths of that part's 64 slots sum to 20480. `slot_of`: in each part, every slot holds exactly one request.
All inputs are finite; a program needn't handle non-finite values. No bound on the sum of `lengths` on one device may be relied on, other than what follows from the above.
Results may differ from the reference program's by a relative error of at most 0.0095.
Values may be sent and summed in bfloat16 or wider, within the bound.
A program may use at most 128 MiB of HBM per device.

```python
import math
import jax
import jax.numpy as jnp
import numpy as np
from jax import lax

D = 8192
FF = 14336
H = 64
KVH = 8
HD = 128
STEPS = 2
CAP = 640
REQ = 64


def draw_incoming(key, part):
    column = jnp.arange(D, dtype=jnp.float32) / D
    background = jnp.clip(jax.random.normal(key, (REQ, STEPS, D), jnp.float32), -6.0, 6.0)
    return (background * 3.0 ** column).astype(jnp.bfloat16)


def draw_queries(key, part):
    return jnp.clip(jax.random.normal(key, (REQ, STEPS, H * HD), jnp.float32), -6.0, 6.0).astype(jnp.bfloat16)


def draw_cache(key, part):
    return jnp.clip(jax.random.normal(key, (REQ, CAP, KVH * 2 * HD), jnp.float32), -6.0, 6.0).astype(jnp.bfloat16)


def steps_of(rng, extent, pieces, least, largest):
    level, own = 1.0, jax.random.fold_in(rng, 6)
    for axis_at, blocks in pieces:
        heights = jnp.exp(jax.random.uniform(jax.random.fold_in(own, axis_at), (blocks,), jnp.float32, least / len(pieces), largest / len(pieces)))
        level = level * jnp.repeat(heights, extent[axis_at] // blocks).reshape([-1 if axis == axis_at else 1 for axis in range(len(extent))])
    return level


def length_profile(number_of, total, reach, skew):
    loads = [(1 << 20) // math.isqrt(grade ** skew) + 1 for grade in range(2, number_of + 1)]
    rest, counts = total - reach - (number_of - 1), [1] * (number_of - 1)
    while rest > 0:
        candidates = [i for i in range(number_of - 1) if counts[i] < reach]
        mass, left = sum([loads[i] for i in candidates]), rest
        for i in candidates:
            addition = min(reach - counts[i], max(1, left * loads[i] // mass), rest)
            counts[i] = counts[i] + addition
            rest = rest - addition
    return np.array([reach] + counts)


def ragged(rng, amount, total, most, slope):
    if amount == 2:
        one = jax.random.randint(rng, (), max(1, total - most), min(most, total - 1) + 1)
        return jnp.stack([one, total - one])
    tallies = jnp.asarray(length_profile(amount, total, most, slope), jnp.int32)
    pairs = (amount - 1) // 2
    source_of, receiver = tallies[1:1 + 2 * pairs:2], tallies[2:2 + 2 * pairs:2]
    margin = jnp.minimum(source_of - 1, most - receiver)
    moved = jax.random.randint(jax.random.fold_in(rng, 1), (pairs,), 0, 1 << 20) % (margin + 1)
    tallies = tallies.at[1:1 + 2 * pairs:2].set(source_of - moved).at[2:2 + 2 * pairs:2].set(receiver + moved)
    return tallies[jax.random.permutation(jax.random.fold_in(rng, 2), amount)]


def scatter_about(stream_key, shape, width, limit, shards=(), kind=jnp.bfloat16):
    values = width * jax.random.normal(stream_key, shape, jnp.float32)
    if shards:
        values = values * steps_of(stream_key, shape, shards, -0.22, 0.18)
    return jnp.clip(values, -limit, limit).astype(kind)


def setup_inputs(seed: int = 0, part: int = 0) -> dict:
    streams_of = jax.random.split(jax.random.key(seed), 12)
    part_keys = jax.random.split(jax.random.fold_in(streams_of[11], part), 12)
    incoming = draw_incoming(jax.random.fold_in(jax.random.fold_in(streams_of[11], part), 71), part)
    queries = draw_queries(jax.random.fold_in(jax.random.fold_in(streams_of[11], part), 71), part)
    new_kv = scatter_about(part_keys[2], (REQ, STEPS, KVH * 2 * HD), 1.0, 6.0, ((0, 4), (2, 4)))
    cache = draw_cache(jax.random.fold_in(jax.random.fold_in(streams_of[11], part), 71), part)
    lengths = ragged(part_keys[4], REQ, REQ * CAP // 2, CAP, 2).astype(jnp.int32)
    slot_of = jax.random.permutation(part_keys[5], REQ).astype(jnp.int32)
    w_out = scatter_about(streams_of[6], (H * HD, D), (H * HD) ** -0.5, 0.0625, ((0, 4), (1, 4)))
    norm_gain = jnp.clip(1.0 + 0.1 * jax.random.normal(streams_of[7], (D,), jnp.float32), 0.5, 1.5)
    w_gate = scatter_about(streams_of[8], (D, FF), D ** -0.5, 0.0625, ((0, 4), (1, 4)))
    w_up = scatter_about(streams_of[9], (D, FF), D ** -0.5, 0.0625, ((0, 4), (1, 4)))
    w_down = scatter_about(streams_of[10], (FF, D), FF ** -0.5, 0.046875, ((0, 4), (1, 4)))
    return {"incoming": incoming, "queries": queries, "new_kv": new_kv, "cache": cache, "lengths": lengths, "slot_of": slot_of, "w_out": w_out, "norm_gain": norm_gain, "w_gate": w_gate, "w_up": w_up, "w_down": w_down}


epsilon = 1e-05

def attend_request(query_rows, fresh_rows, kept_rows, length):
    groups = H // KVH
    score_scale = HD ** (-0.5)
    query_wide = query_rows.astype(jnp.float32).reshape(STEPS, KVH, groups, HD)
    kept_wide = kept_rows.astype(jnp.float32).reshape(CAP, KVH, 2, HD)
    fresh_wide = fresh_rows.astype(jnp.float32).reshape(STEPS, KVH, 2, HD)
    kept_scores = jnp.einsum('skgd,ckd->skgc', query_wide, kept_wide[:, :, 0]) * score_scale
    in_range = jnp.arange(CAP) < length
    kept_scores = jnp.where(in_range, kept_scores, -jnp.inf)
    fresh_scores = jnp.einsum('skgd,tkd->skgt', query_wide, fresh_wide[:, :, 0]) * score_scale
    causal = jnp.arange(STEPS)[None, :] <= jnp.arange(STEPS)[:, None]
    fresh_scores = jnp.where(causal[:, None, None, :], fresh_scores, -jnp.inf)
    top_score = jnp.maximum(lax.optimization_barrier(jnp.max(kept_scores, -1)), lax.optimization_barrier(jnp.max(fresh_scores, -1)))
    kept_exp = jnp.exp(kept_scores - top_score[..., None])
    fresh_exp = jnp.exp(fresh_scores - top_score[..., None])
    denominator = lax.optimization_barrier(jnp.sum(kept_exp, -1)) + lax.optimization_barrier(jnp.sum(fresh_exp, -1))
    kept_prob = (kept_exp / denominator[..., None]).astype(jnp.bfloat16)
    fresh_prob = (fresh_exp / denominator[..., None]).astype(jnp.bfloat16)
    mixture = jnp.einsum('skgc,ckd->skgd', kept_prob.astype(jnp.float32), kept_wide[:, :, 1])
    mixture = mixture + jnp.einsum('skgt,tkd->skgd', fresh_prob.astype(jnp.float32), fresh_wide[:, :, 1])
    return mixture.astype(jnp.bfloat16).reshape(STEPS, H * HD)

def reference(incoming, queries, new_kv, cache, lengths, slot_of, w_out, norm_gain, w_gate, w_up, w_down):

    def attend_one(request):
        slot_index = slot_of[request]
        return attend_request(queries[request], new_kv[request], cache[slot_index], lengths[slot_index])
    attended = lax.map(attend_one, jnp.arange(REQ, dtype=jnp.int32))
    flattened = attended.reshape(REQ * STEPS, H * HD)
    heads_out = jnp.dot(flattened, w_out, preferred_element_type=jnp.float32)
    residual = (incoming.reshape(REQ * STEPS, D).astype(jnp.float32) + heads_out).astype(jnp.bfloat16)
    residual_wide = residual.astype(jnp.float32)
    squares = lax.optimization_barrier(jnp.sum(residual_wide * residual_wide, -1, keepdims=True))
    normed = (residual_wide * lax.rsqrt(squares / D + epsilon) * norm_gain.astype(jnp.float32)).astype(jnp.bfloat16)
    gate = jnp.dot(normed, w_gate, preferred_element_type=jnp.float32)
    upward = jnp.dot(normed, w_up, preferred_element_type=jnp.float32)
    hidden = (jax.nn.silu(gate) * upward).astype(jnp.bfloat16)
    lowered = jnp.dot(hidden, w_down, preferred_element_type=jnp.float32)
    return (residual_wide + lowered).astype(jnp.bfloat16).reshape(REQ, STEPS, D)
```

```python
import functools

import jax
import jax.numpy as jnp
from jax import lax
from jax.experimental import pallas as pl
from jax.experimental.pallas import tpu as pltpu
from jax.sharding import PartitionSpec as P

D = 8192
H = 64
KVH = 8
HD = 128
STEPS = 2
CAP = 640


epsilon = 1e-05
TILE = 512
MESH = pl.DeviceIdType.MESH


def tail_kernel(
    cfg, attended, incoming, gain, wo, wg, wu, wd, out,
    wo_v, wg_v, wu_v, wd_v,
    fa, pa, oa, ra, res, h, ss, ssr,
    fg, s1, o1, r1, s2, o2, r2, hb,
    pd, od, rd,
    wo_s, wg_s, wu_s, wd_s,
    a_ss, a_rs, b_ss, b_rs, q_ss, q_rs,
    c1_ss, c1_rs, c2_ss, c2_rs,
    hp_ss, hp_rs, hx_ss, hx_rs, hf_ss, hf_rs,
    d_ss, d_rs,
):
    Z, RB, T, NA, NF = cfg
    A = 4
    z = lax.axis_index("ffn")
    a = lax.axis_index("att")
    x, c = a // 2, a % 2
    partner = 2 * x + (1 - c)
    xpeer = 2 * (1 - x) + c
    bf, f32 = jnp.bfloat16, jnp.float32

    def wcopy(src, dst, sem, k):
        return pltpu.make_async_copy(
            src.at[:, pl.ds(pl.multiple_of(k * T, T), T)], dst.at[k], sem.at[k]
        )

    for k in range(NA):
        wcopy(wo, wo_v, wo_s, k).start()
    for k in range(NF):
        wcopy(wg, wg_v, wg_s, k).start()
        wcopy(wu, wu_v, wu_s, k).start()
    for k in range(NA):
        wcopy(wd, wd_v, wd_s, k).start()

    barrier = pltpu.get_barrier_semaphore()
    for d in range(1, Z):
        pl.semaphore_signal(barrier, 1, device_id={"ffn": (z + d) % Z}, device_id_type=MESH)
    for d in range(1, A):
        pl.semaphore_signal(barrier, 1, device_id={"att": (a + d) % A}, device_id_type=MESH)
    pl.semaphore_wait(barrier, Z - 1 + A - 1)

    def remote(src, dst, ss_, rs_, axis, peer):
        return pltpu.make_async_remote_copy(
            src_ref=src, dst_ref=dst, send_sem=ss_, recv_sem=rs_,
            device_id={axis: peer}, device_id_type=MESH,
        )

    def a_copy(k, d):
        peer = (z + d) % Z
        return remote(pa.at[k, peer], ra.at[k, d - 1], a_ss.at[k, d - 1], a_rs.at[k, d - 1], "ffn", peer)

    def b_copy(k, d):
        peer = (z + d) % Z
        return remote(res.at[k, z], res.at[k, z], b_ss.at[k, d - 1], b_rs.at[k, d - 1], "ffn", peer)

    def b_wait(k, d):
        origin = (z + Z - d) % Z
        remote(res.at[k, origin], res.at[k, origin], b_ss.at[k, d - 1], b_rs.at[k, d - 1], "ffn", origin).wait_recv()

    def q_copy(d):
        peer = (a + d) % A
        return remote(ss.at[peer], ssr.at[d - 1], q_ss.at[d - 1], q_rs.at[d - 1], "att", peer)

    def c1_copy(k):
        return remote(s1.at[k], r1.at[k], c1_ss.at[k], c1_rs.at[k], "att", partner)

    def c2_copy(k):
        return remote(s2.at[k], r2.at[k], c2_ss.at[k], c2_rs.at[k], "att", xpeer)

    def hp_copy(k, block):
        return remote(hb.at[k, block], hb.at[k, block], hp_ss.at[k], hp_rs.at[k], "att", partner)

    def hx_copy(k, block):
        return remote(hb.at[k, block], hb.at[k, block], hx_ss.at[k], hx_rs.at[k], "att", xpeer)

    def hf_copy(k, block):
        return remote(hb.at[k, block], hb.at[k, block], hf_ss.at[k], hf_rs.at[k], "att", partner)

    def d_copy(k, d):
        peer = (z + d) % Z
        return remote(pd.at[k, peer], rd.at[k, d - 1], d_ss.at[k, d - 1], d_rs.at[k, d - 1], "ffn", peer)

    @pl.loop(0, NA)
    def _(k):
        wcopy(wo, wo_v, wo_s, k).wait()
        p = jnp.dot(attended[...], wo_v[k], preferred_element_type=f32).reshape(Z, RB, T)
        fa[...] = p
        pa[k] = p.astype(bf)
        oa[k] = fa[z]
        for d in range(1, Z):
            a_copy(k, d).start()

    for k in range(NA):
        total = incoming[z, :, k * T:(k + 1) * T].astype(f32) + oa[k]
        for d in range(1, Z):
            a_copy(k, d).wait_recv()
            total = total + ra[k, d - 1].astype(f32)
        res[k, z] = total.astype(bf)
        for d in range(1, Z):
            b_copy(k, d).start()

    squares = jnp.zeros((Z, RB, 1), f32)
    for k in range(NA):
        for d in range(1, Z):
            b_wait(k, d)
        wide = res[k].astype(f32)
        squares = squares + jnp.sum(wide * wide, -1, keepdims=True)
        h[:, k * T:(k + 1) * T] = (
            (wide * gain[:, k * T:(k + 1) * T]).astype(bf).reshape(Z * RB, T)
        )
    ss[...] = jnp.broadcast_to(squares.reshape(A, ss.shape[1], 1), ss.shape)
    for d in range(1, A):
        q_copy(d).start()

    def first(k):
        wcopy(wg, wg_v, wg_s, k).wait()
        wcopy(wu, wu_v, wu_s, k).wait()
        for i, w in enumerate((wg_v, wu_v)):
            p = jnp.dot(h[...], w[k], preferred_element_type=f32)
            fg[i] = p.reshape(fg.shape[1:])
            for xx in range(2):
                s1[k, i, xx] = fg[i, 2 * xx + (1 - c)].astype(bf)
                o1[k, i, xx] = fg[i, 2 * xx + c]
        c1_copy(k).start()

    def second(k):
        c1_copy(k).wait_recv()
        for i in range(2):
            s2[k, i] = (o1[k, i, 1 - x] + r1[k, i, 1 - x].astype(f32)).astype(bf)
            o2[k, i] = o1[k, i, x] + r1[k, i, x].astype(f32)
        c2_copy(k).start()

    first(0)

    @pl.loop(1, NF)
    def _(k):
        first(k)
        second(k - 1)

    second(NF - 1)

    total_squares = ss[a]
    for d in range(1, A):
        q_copy(d).wait_recv()
        total_squares = total_squares + ssr[d - 1]
    inverse = lax.rsqrt(total_squares / D + epsilon)[:, :1]

    @pl.loop(0, NF)
    def _(k):
        c2_copy(k).wait_recv()
        gate = (o2[k, 0] + r2[k, 0].astype(f32)) * inverse
        up = (o2[k, 1] + r2[k, 1].astype(f32)) * inverse
        hb[k, a] = (gate / (1.0 + jnp.exp(-gate)) * up).astype(bf)
        hx_copy(k, a).start()
        hp_copy(k, a).start()

    @pl.loop(0, NF)
    def _(k):
        hx_copy(k, xpeer).wait_recv()
        hf_copy(k, xpeer).start()

    @pl.loop(0, NF)
    def _(k):
        hp_copy(k, partner).wait_recv()
        hf_copy(k, 2 * (1 - x) + (1 - c)).wait_recv()

    @pl.loop(0, NA)
    def _(n):
        wcopy(wd, wd_v, wd_s, n).wait()
        p = jnp.zeros((Z * RB, T), f32)
        for k in range(NF):
            p = p + jnp.dot(
                hb[k].reshape(Z * RB, T), wd_v[n, k * T:(k + 1) * T, :], preferred_element_type=f32
            )
        p = p.reshape(Z, RB, T)
        fa[...] = p
        pd[n] = p.astype(bf)
        od[n] = fa[z]
        for d in range(1, Z):
            d_copy(n, d).start()

    for n in range(NA):
        total = res[n, z].astype(f32) + od[n]
        for d in range(1, Z):
            d_copy(n, d).wait_recv()
            total = total + rd[n, d - 1].astype(f32)
        out[:, n * T:(n + 1) * T] = total.astype(bf)

    for k in range(NA):
        for d in range(1, Z):
            a_copy(k, d).wait_send()
            b_copy(k, d).wait_send()
            d_copy(k, d).wait_send()
    for d in range(1, A):
        q_copy(d).wait_send()
    for k in range(NF):
        c1_copy(k).wait_send()
        c2_copy(k).wait_send()
        hp_copy(k, a).wait_send()
        hx_copy(k, a).wait_send()
        hf_copy(k, xpeer).wait_send()


def tail(attended, incoming, gain, w_out, w_gate, w_up, w_down):
    Z = lax.axis_size("ffn")
    rows, kdim = attended.shape
    width = w_out.shape[1]
    units = w_gate.shape[1]
    RB, T = rows // Z, TILE
    NA, NF = width // T, units // T
    AB = rows // 4
    bf, f32 = jnp.bfloat16, jnp.float32
    V = pltpu.VMEM
    dma = pltpu.SemaphoreType.DMA
    vm = pl.BlockSpec(memory_space=pltpu.VMEM)
    hbm = pl.BlockSpec(memory_space=pl.ANY)
    scratch = [
        V((NA, kdim, T), bf), V((NF, width, T), bf), V((NF, width, T), bf), V((NA, units, T), bf),
        V((Z, RB, T), f32), V((NA, Z, RB, T), bf), V((NA, RB, T), f32), V((NA, Z - 1, RB, T), bf),
        V((NA, Z, RB, T), bf), V((rows, width), bf), V((4, AB, 128), f32), V((3, AB, 128), f32),
        V((2, 4, AB, T), f32), V((NF, 2, 2, AB, T), bf), V((NF, 2, 2, AB, T), f32),
        V((NF, 2, 2, AB, T), bf), V((NF, 2, AB, T), bf), V((NF, 2, AB, T), f32),
        V((NF, 2, AB, T), bf), V((NF, 4, AB, T), bf),
        V((NA, Z, RB, T), bf), V((NA, RB, T), f32), V((NA, Z - 1, RB, T), bf),
        dma((NA,)), dma((NF,)), dma((NF,)), dma((NA,)),
        dma((NA, Z - 1)), dma((NA, Z - 1)), dma((NA, Z - 1)), dma((NA, Z - 1)), dma((3,)), dma((3,)),
    ] + [dma((NF,)) for _ in range(10)] + [dma((NA, Z - 1)), dma((NA, Z - 1))]
    return pl.pallas_call(
        functools.partial(tail_kernel, (Z, RB, T, NA, NF)),
        out_shape=jax.ShapeDtypeStruct((RB, width), bf),
        in_specs=[vm, vm, vm, hbm, hbm, hbm, hbm],
        out_specs=vm,
        scratch_shapes=scratch,
        compiler_params=pltpu.CompilerParams(
            collective_id=1, has_side_effects=True, vmem_limit_bytes=67043328
        ),
    )(attended, incoming, gain, w_out, w_gate, w_up, w_down)


def local(
    incoming, queries, new_kv, cache, lengths, slot_of, w_out, norm_gain, w_gate, w_up, w_down
):
    ffn_count = lax.axis_size("ffn")
    fast = lax.axis_size("att") == 4 and slot_of.shape[0] * STEPS <= 128
    att_index = lax.axis_index("att")
    ffn_index = lax.axis_index("ffn")
    request_count = slot_of.shape[0]
    slot_count = cache.shape[0]
    kv_local = cache.shape[2] // (2 * HD)
    groups = H // KVH
    score_scale = HD ** (-0.5)
    gathered_q, gathered_kv = (
        lax.all_gather(queries, "att", axis=0, tiled=True),
        lax.all_gather(new_kv, "att", axis=0, tiled=True),
    )
    holders = (
        jnp.zeros((request_count,), jnp.int32)
        .at[slot_of]
        .set(jnp.arange(request_count, dtype=jnp.int32))
    )
    my_requests = lax.dynamic_slice_in_dim(holders, att_index * slot_count, slot_count)
    query_mine = jnp.take(gathered_q, my_requests, axis=0).reshape(
        slot_count, STEPS, kv_local, groups, HD
    )
    fresh_mine = jnp.take(gathered_kv, my_requests, axis=0).reshape(
        slot_count, STEPS, kv_local, 2, HD
    )
    cache_view = cache.reshape(slot_count, CAP, kv_local, 2, HD)
    fresh_scores = (
        jnp.einsum(
            "rskgd,rtkd->rskgt",
            query_mine,
            fresh_mine[:, :, :, 0],
            preferred_element_type=jnp.float32,
        )
        * score_scale
    )
    causal = jnp.arange(STEPS)[None, :] <= jnp.arange(STEPS)[:, None]
    fresh_scores = jnp.where(causal[None, :, None, None, :], fresh_scores, -jnp.inf)
    kept_scores = (
        jnp.einsum(
            "rskgd,rckd->rskgc",
            query_mine,
            cache_view[:, :, :, 0],
            preferred_element_type=jnp.float32,
        )
        * score_scale
    )
    in_range = jnp.arange(CAP)[None, :] < lengths[:, None]
    kept_scores = jnp.where(in_range[:, None, None, None, :], kept_scores, -jnp.inf)
    top_score = jnp.maximum(jnp.max(kept_scores, -1), jnp.max(fresh_scores, -1))
    kept_exp = jnp.exp(kept_scores - top_score[..., None])
    fresh_exp = jnp.exp(fresh_scores - top_score[..., None])
    denominator = jnp.sum(kept_exp, -1) + jnp.sum(fresh_exp, -1)
    kept_prob = (kept_exp / denominator[..., None]).astype(jnp.bfloat16)
    fresh_prob = (fresh_exp / denominator[..., None]).astype(jnp.bfloat16)
    mixture = jnp.einsum(
        "rskgc,rckd->rskgd", kept_prob, cache_view[:, :, :, 1], preferred_element_type=jnp.float32
    )
    mixture = mixture + jnp.einsum(
        "rskgt,rtkd->rskgd", fresh_prob, fresh_mine[:, :, :, 1], preferred_element_type=jnp.float32
    )
    attended = mixture.astype(jnp.bfloat16).reshape(slot_count, STEPS, kv_local * groups * HD)
    shard_rows = lax.all_gather(attended, "att", axis=0, tiled=True)
    row_count = shard_rows.shape[0]
    flattened = shard_rows.reshape(row_count * STEPS, shard_rows.shape[2])
    if fast:
        own = tail(
            jnp.take(shard_rows, slot_of, axis=0).reshape(row_count * STEPS, -1),
            incoming.reshape(ffn_count, -1, incoming.shape[2]),
            norm_gain[None],
            w_out,
            w_gate,
            w_up,
            w_down,
        )
        return own.reshape(-1, STEPS, incoming.shape[2])
    heads_slots = jnp.dot(flattened, w_out, preferred_element_type=jnp.float32).reshape(
        row_count, STEPS, w_out.shape[1]
    )
    heads_requests = jnp.take(heads_slots, slot_of, axis=0)
    heads_total = lax.psum(heads_requests, "ffn")
    residual = (incoming.astype(jnp.float32) + heads_total).astype(jnp.bfloat16)
    residual_wide = residual.astype(jnp.float32)
    squares = lax.psum(jnp.sum(residual_wide * residual_wide, -1), "att")
    normed = (residual_wide * lax.rsqrt(squares / D + epsilon)[..., None] * norm_gain).astype(
        jnp.bfloat16
    )
    normed = normed.reshape(request_count * STEPS, normed.shape[2])
    gate_term = jnp.dot(normed, w_gate, preferred_element_type=jnp.float32)
    upward_term = jnp.dot(normed, w_up, preferred_element_type=jnp.float32)
    unit_share = lax.psum_scatter(
        jnp.concatenate([gate_term, upward_term], 1), "att", scatter_dimension=0, tiled=True
    )
    unit_width = w_gate.shape[1]
    hidden_share = (jax.nn.silu(unit_share[:, :unit_width]) * unit_share[:, unit_width:]).astype(
        jnp.bfloat16
    )
    down_part = jnp.dot(
        lax.all_gather(hidden_share, "att", axis=0, tiled=True),
        w_down,
        preferred_element_type=jnp.float32,
    )
    out_share = lax.psum_scatter(down_part, "ffn", scatter_dimension=0, tiled=True)
    row_share = request_count // ffn_count
    own_state = lax.dynamic_slice_in_dim(residual_wide, ffn_index * row_share, row_share, 0)
    return (own_state + out_share.reshape(row_share, STEPS, out_share.shape[1])).astype(
        jnp.bfloat16
    )


def solution(mesh):
    return jax.shard_map(
        local,
        mesh=mesh,
        in_specs=(
            P("parts", None, "att"),
            P(("parts", "att"), None, "ffn"),
            P(("parts", "att"), None, "ffn"),
            P(("parts", "att"), None, "ffn"),
            P(("parts", "att")),
            P("parts"),
            P("ffn", "att"),
            P("att"),
            P("att", "ffn"),
            P("att", "ffn"),
            P("ffn", "att"),
        ),
        out_specs=P(("parts", "ffn"), None, "att"),
        check_vma=False,
    )
```

```python
import functools

import jax
import jax.numpy as jnp
from jax import lax
from jax.experimental import pallas as pl
from jax.experimental.pallas import tpu as pltpu
from jax.sharding import PartitionSpec as P

D = 8192
H = 64
KVH = 8
HD = 128
STEPS = 2
CAP = 640


epsilon = 1e-05
TILE = 512
MESH = pl.DeviceIdType.MESH


def layer_kernel(
    cfg, holders, lengths, q, kv, place, incoming, gain, cache, wo, wg, wu, wd, out,
    gq, gkv, of, tb, attended,
    wo_v, wg_v, wu_v, wd_v,
    fa, pa, oa, ra, res, h, ss, ssr,
    fg, s1, o1, r1, s2, o2, r2, hb,
    pd, od, rd,
    wo_s, wg_s, wu_s, wd_s,
    a_ss, a_rs, b_ss, b_rs, q_ss, q_rs,
    c1_ss, c1_rs, c2_ss, c2_rs,
    hp_ss, hp_rs, hx_ss, hx_rs, hf_ss, hf_rs,
    d_ss, d_rs,
    cache_s, qp_ss, qp_rs, qx_ss, qx_rs, qf_ss, qf_rs,
    tp_ss, tp_rs, tx_ss, tx_rs, tf_ss, tf_rs,
):
    Z, RB, T, NA, NF = cfg
    S = cache.shape[0]
    kv_local = cache.shape[2] // (2 * HD)
    groups = H // KVH
    QR = STEPS * groups
    per = wd_v.shape[1] // CAP
    A = 4
    z = lax.axis_index("ffn")
    a = lax.axis_index("att")
    x, c = a // 2, a % 2
    partner = 2 * x + (1 - c)
    xpeer = 2 * (1 - x) + c
    bf, f32 = jnp.bfloat16, jnp.float32

    def wcopy(src, dst, sem, k):
        return pltpu.make_async_copy(
            src.at[:, pl.ds(pl.multiple_of(k * T, T), T)], dst.at[k], sem.at[k]
        )

    def kept_rows(i):
        return pl.ds(pl.multiple_of((i % per) * CAP, CAP), CAP)

    def cache_copy(i):
        return pltpu.make_async_copy(cache.at[i], wd_v.at[i // per, kept_rows(i)], cache_s.at[i])

    @pl.loop(0, S)
    def _(i):
        cache_copy(i).start()

    for k in range(NA):
        wcopy(wo, wo_v, wo_s, k).start()
    for k in range(NF):
        wcopy(wg, wg_v, wg_s, k).start()
        wcopy(wu, wu_v, wu_s, k).start()

    barrier = pltpu.get_barrier_semaphore()
    for d in range(1, Z):
        pl.semaphore_signal(barrier, 1, device_id={"ffn": (z + d) % Z}, device_id_type=MESH)
    for d in range(1, A):
        pl.semaphore_signal(barrier, 1, device_id={"att": (a + d) % A}, device_id_type=MESH)
    pl.semaphore_wait(barrier, Z - 1 + A - 1)

    def remote(src, dst, ss_, rs_, axis, peer):
        return pltpu.make_async_remote_copy(
            src_ref=src, dst_ref=dst, send_sem=ss_, recv_sem=rs_,
            device_id={axis: peer}, device_id_type=MESH,
        )

    def a_copy(k, d):
        peer = (z + d) % Z
        return remote(pa.at[k, peer], ra.at[k, d - 1], a_ss.at[k, d - 1], a_rs.at[k, d - 1], "ffn", peer)

    def b_copy(k, d):
        peer = (z + d) % Z
        return remote(res.at[k, z], res.at[k, z], b_ss.at[k, d - 1], b_rs.at[k, d - 1], "ffn", peer)

    def b_wait(k, d):
        origin = (z + Z - d) % Z
        remote(res.at[k, origin], res.at[k, origin], b_ss.at[k, d - 1], b_rs.at[k, d - 1], "ffn", origin).wait_recv()

    def q_copy(d):
        peer = (a + d) % A
        return remote(ss.at[peer], ssr.at[d - 1], q_ss.at[d - 1], q_rs.at[d - 1], "att", peer)

    def c1_copy(k):
        return remote(s1.at[k], r1.at[k], c1_ss.at[k], c1_rs.at[k], "att", partner)

    def c2_copy(k):
        return remote(s2.at[k], r2.at[k], c2_ss.at[k], c2_rs.at[k], "att", xpeer)

    def hp_copy(k, block):
        return remote(hb.at[k, block], hb.at[k, block], hp_ss.at[k], hp_rs.at[k], "att", partner)

    def hx_copy(k, block):
        return remote(hb.at[k, block], hb.at[k, block], hx_ss.at[k], hx_rs.at[k], "att", xpeer)

    def hf_copy(k, block):
        return remote(hb.at[k, block], hb.at[k, block], hf_ss.at[k], hf_rs.at[k], "att", partner)

    def d_copy(k, d):
        peer = (z + d) % Z
        return remote(pd.at[k, peer], rd.at[k, d - 1], d_ss.at[k, d - 1], d_rs.at[k, d - 1], "ffn", peer)

    def block_of(ref, owner):
        return ref.at[pl.ds(owner * S, S)]

    for i, (mine, everyone) in enumerate(((q, gq), (kv, gkv))):
        remote(mine, block_of(everyone, a), qx_ss.at[i], qx_rs.at[i], "att", xpeer).start()
        remote(mine, block_of(everyone, a), qp_ss.at[i], qp_rs.at[i], "att", partner).start()
        everyone[pl.ds(a * S, S)] = mine[...]

    def qf_copy(i, everyone):
        block = block_of(everyone, xpeer)
        return remote(block, block, qf_ss.at[i], qf_rs.at[i], "att", partner)

    far = 2 * (1 - x) + (1 - c)
    for i, (mine, everyone) in enumerate(((q, gq), (kv, gkv))):
        remote(mine, block_of(everyone, xpeer), qx_ss.at[i], qx_rs.at[i], "att", xpeer).wait_recv()
        qf_copy(i, everyone).start()
    for i, (mine, everyone) in enumerate(((q, gq), (kv, gkv))):
        remote(mine, block_of(everyone, partner), qp_ss.at[i], qp_rs.at[i], "att", partner).wait_recv()
        block = block_of(everyone, far)
        remote(block, block, qf_ss.at[i], qf_rs.at[i], "att", partner).wait_recv()

    def attend(i, g):
        holder, length = holders[i], lengths[i]
        rows = gq[holder][g * QR:(g + 1) * QR]
        fresh = gkv[holder].astype(f32)
        kept = kept_rows(i)
        keys = wd_v[i // per, kept, g * 2 * HD:(g * 2 + 1) * HD]
        values = wd_v[i // per, kept, (g * 2 + 1) * HD:(g * 2 + 2) * HD]
        scale = HD ** (-0.5)
        scores = lax.dot_general(
            rows, keys, (((1,), (1,)), ((), ())), preferred_element_type=f32
        ) * scale
        column = lax.broadcasted_iota(jnp.int32, scores.shape, 1)
        scores = jnp.where(column < length, scores, -jnp.inf)
        wide = rows.astype(f32)
        step = lax.broadcasted_iota(jnp.int32, (QR, 1), 0) // groups
        new_scores = []
        for t in range(STEPS):
            at = g * 2 * STEPS + t
            score = jnp.sum(wide * fresh[at:at + 1], -1, keepdims=True) * scale
            new_scores.append(jnp.where(step >= t, score, -jnp.inf))
        top = jnp.max(scores, -1, keepdims=True)
        for score in new_scores:
            top = jnp.maximum(top, score)
        weights = jnp.exp(scores - top)
        total = jnp.sum(weights, -1, keepdims=True)
        new_weights = [jnp.exp(score - top) for score in new_scores]
        for weight in new_weights:
            total = total + weight
        mixed = jnp.dot((weights / total).astype(bf), values, preferred_element_type=f32)
        for t in range(STEPS):
            at = g * 2 * STEPS + STEPS + t
            mixed = mixed + (new_weights[t] / total).astype(bf).astype(f32) * fresh[at:at + 1]
        of[pl.ds(pl.multiple_of(i * QR, QR), QR), :] = mixed

    def t_copy(k, ss_, rs_, block, peer):
        return remote(tb.at[k, block], tb.at[k, block], ss_.at[k], rs_.at[k], "att", peer)

    heads = T // HD
    chunks = groups // heads
    for g in range(kv_local):
        @pl.loop(0, S // 4)
        def _(j):
            for n in range(4):
                if g == 0:
                    cache_copy(j * 4 + n).wait()
            for n in range(4):
                attend(j * 4 + n, g)

        for k in range(chunks):
            for t in range(STEPS):
                for n in range(heads):
                    row = t * groups + k * heads + n
                    tb[g * chunks + k, a, t * S:(t + 1) * S, n * HD:(n + 1) * HD] = of[
                        pl.ds(row, S, stride=QR), :
                    ].astype(bf)
            t_copy(g * chunks + k, tx_ss, tx_rs, a, xpeer).start()
            t_copy(g * chunks + k, tp_ss, tp_rs, a, partner).start()

    for k in range(NA):
        wcopy(wd, wd_v, wd_s, k).start()
    for k in range(NA):
        t_copy(k, tx_ss, tx_rs, xpeer, xpeer).wait_recv()
        t_copy(k, tf_ss, tf_rs, xpeer, partner).start()
    for k in range(NA):
        t_copy(k, tp_ss, tp_rs, partner, partner).wait_recv()
        t_copy(k, tf_ss, tf_rs, far, partner).wait_recv()
        attended[:, k * T:(k + 1) * T] = jnp.dot(
            place[...], tb[k].reshape(Z * RB, T), preferred_element_type=f32
        ).astype(bf)

    @pl.loop(0, NA)
    def _(k):
        wcopy(wo, wo_v, wo_s, k).wait()
        p = jnp.dot(attended[...], wo_v[k], preferred_element_type=f32).reshape(Z, RB, T)
        fa[...] = p
        pa[k] = p.astype(bf)
        oa[k] = fa[z]
        for d in range(1, Z):
            a_copy(k, d).start()

    for k in range(NA):
        total = incoming[:, k * T:(k + 1) * T].astype(f32) + oa[k]
        for d in range(1, Z):
            a_copy(k, d).wait_recv()
            total = total + ra[k, d - 1].astype(f32)
        res[k, z] = total.astype(bf)
        for d in range(1, Z):
            b_copy(k, d).start()

    squares = jnp.zeros((Z, RB, 1), f32)
    for k in range(NA):
        for d in range(1, Z):
            b_wait(k, d)
        wide = res[k].astype(f32)
        squares = squares + jnp.sum(wide * wide, -1, keepdims=True)
        h[:, k * T:(k + 1) * T] = (
            (wide * gain[:, k * T:(k + 1) * T]).astype(bf).reshape(Z * RB, T)
        )
    ss[...] = jnp.broadcast_to(squares.reshape(A, ss.shape[1], 1), ss.shape)
    for d in range(1, A):
        q_copy(d).start()

    def first(k):
        wcopy(wg, wg_v, wg_s, k).wait()
        wcopy(wu, wu_v, wu_s, k).wait()
        for i, w in enumerate((wg_v, wu_v)):
            p = jnp.dot(h[...], w[k], preferred_element_type=f32)
            fg[i] = p.reshape(fg.shape[1:])
            for xx in range(2):
                s1[k, i, xx] = fg[i, 2 * xx + (1 - c)].astype(bf)
                o1[k, i, xx] = fg[i, 2 * xx + c]
        c1_copy(k).start()

    def second(k):
        c1_copy(k).wait_recv()
        for i in range(2):
            s2[k, i] = (o1[k, i, 1 - x] + r1[k, i, 1 - x].astype(f32)).astype(bf)
            o2[k, i] = o1[k, i, x] + r1[k, i, x].astype(f32)
        c2_copy(k).start()

    first(0)

    @pl.loop(1, NF)
    def _(k):
        first(k)
        second(k - 1)

    second(NF - 1)

    total_squares = ss[a]
    for d in range(1, A):
        q_copy(d).wait_recv()
        total_squares = total_squares + ssr[d - 1]
    inverse = lax.rsqrt(total_squares / D + epsilon)[:, :1]

    @pl.loop(0, NF)
    def _(k):
        c2_copy(k).wait_recv()
        gate = (o2[k, 0] + r2[k, 0].astype(f32)) * inverse
        up = (o2[k, 1] + r2[k, 1].astype(f32)) * inverse
        hb[k, a] = (gate / (1.0 + jnp.exp(-gate)) * up).astype(bf)
        hx_copy(k, a).start()
        hp_copy(k, a).start()

    @pl.loop(0, NF)
    def _(k):
        hx_copy(k, xpeer).wait_recv()
        hf_copy(k, xpeer).start()

    @pl.loop(0, NF)
    def _(k):
        hp_copy(k, partner).wait_recv()
        hf_copy(k, 2 * (1 - x) + (1 - c)).wait_recv()

    @pl.loop(0, NA)
    def _(n):
        wcopy(wd, wd_v, wd_s, n).wait()
        p = jnp.zeros((Z * RB, T), f32)
        for k in range(NF):
            p = p + jnp.dot(
                hb[k].reshape(Z * RB, T), wd_v[n, k * T:(k + 1) * T, :], preferred_element_type=f32
            )
        p = p.reshape(Z, RB, T)
        fa[...] = p
        pd[n] = p.astype(bf)
        od[n] = fa[z]
        for d in range(1, Z):
            d_copy(n, d).start()

    for n in range(NA):
        total = res[n, z].astype(f32) + od[n]
        for d in range(1, Z):
            d_copy(n, d).wait_recv()
            total = total + rd[n, d - 1].astype(f32)
        out[:, n * T:(n + 1) * T] = total.astype(bf)

    for k in range(NA):
        for d in range(1, Z):
            a_copy(k, d).wait_send()
            b_copy(k, d).wait_send()
            d_copy(k, d).wait_send()
    for d in range(1, A):
        q_copy(d).wait_send()
    for i, (mine, everyone) in enumerate(((q, gq), (kv, gkv))):
        remote(mine, block_of(everyone, a), qx_ss.at[i], qx_rs.at[i], "att", xpeer).wait_send()
        remote(mine, block_of(everyone, a), qp_ss.at[i], qp_rs.at[i], "att", partner).wait_send()
        qf_copy(i, everyone).wait_send()
    for k in range(NA):
        t_copy(k, tx_ss, tx_rs, a, xpeer).wait_send()
        t_copy(k, tp_ss, tp_rs, a, partner).wait_send()
        t_copy(k, tf_ss, tf_rs, xpeer, partner).wait_send()
    for k in range(NF):
        c1_copy(k).wait_send()
        c2_copy(k).wait_send()
        hp_copy(k, a).wait_send()
        hx_copy(k, a).wait_send()
        hf_copy(k, xpeer).wait_send()


def fused(holders, lengths, q, kv, place, incoming, gain, cache, w_out, w_gate, w_up, w_down):
    Z = lax.axis_size("ffn")
    rows, kdim = place.shape[0], w_out.shape[0]
    width = w_out.shape[1]
    units = w_gate.shape[1]
    RB, T = rows // Z, TILE
    NA, NF = width // T, units // T
    AB = rows // 4
    S = cache.shape[0]
    bf, f32 = jnp.bfloat16, jnp.float32
    V = pltpu.VMEM
    dma = pltpu.SemaphoreType.DMA
    vm = pl.BlockSpec(memory_space=pltpu.VMEM)
    sm = pl.BlockSpec(memory_space=pltpu.SMEM)
    hbm = pl.BlockSpec(memory_space=pl.ANY)
    scratch = [
        V((4 * S,) + q.shape[1:], bf), V((4 * S,) + kv.shape[1:], bf),
        V((S * STEPS * (H // KVH), HD), f32), V((kdim // T, 4, AB, T), bf), V((rows, kdim), bf),
        V((NA, kdim, T), bf), V((NF, width, T), bf), V((NF, width, T), bf), V((NA, units, T), bf),
        V((Z, RB, T), f32), V((NA, Z, RB, T), bf), V((NA, RB, T), f32), V((NA, Z - 1, RB, T), bf),
        V((NA, Z, RB, T), bf), V((rows, width), bf), V((4, AB, 128), f32), V((3, AB, 128), f32),
        V((2, 4, AB, T), f32), V((NF, 2, 2, AB, T), bf), V((NF, 2, 2, AB, T), f32),
        V((NF, 2, 2, AB, T), bf), V((NF, 2, AB, T), bf), V((NF, 2, AB, T), f32),
        V((NF, 2, AB, T), bf), V((NF, 4, AB, T), bf),
        V((NA, Z, RB, T), bf), V((NA, RB, T), f32), V((NA, Z - 1, RB, T), bf),
        dma((NA,)), dma((NF,)), dma((NF,)), dma((NA,)),
        dma((NA, Z - 1)), dma((NA, Z - 1)), dma((NA, Z - 1)), dma((NA, Z - 1)), dma((3,)), dma((3,)),
    ] + [dma((NF,)) for _ in range(10)] + [dma((NA, Z - 1)), dma((NA, Z - 1))]
    scratch += [dma((S,))] + [dma((2,)) for _ in range(6)] + [dma((NA,)) for _ in range(6)]
    return pl.pallas_call(
        functools.partial(layer_kernel, (Z, RB, T, NA, NF)),
        out_shape=jax.ShapeDtypeStruct((RB, width), bf),
        in_specs=[sm, sm, vm, vm, vm, vm, vm, hbm, hbm, hbm, hbm, hbm],
        out_specs=vm,
        scratch_shapes=scratch,
        compiler_params=pltpu.CompilerParams(
            collective_id=1, has_side_effects=True, vmem_limit_bytes=67043328
        ),
    )(holders, lengths, q, kv, place, incoming, gain, cache, w_out, w_gate, w_up, w_down)


def fits(queries, cache, w_out, w_gate, slot_of):
    slots = cache.shape[0]
    chunks = w_out.shape[1] // TILE
    return (
        lax.axis_size("att") == 4
        and lax.axis_size("ffn") == 4
        and slots % 16 == 0
        and slot_of.shape[0] == 4 * slots
        and slot_of.shape[0] * STEPS <= 128
        and cache.shape[2] == TILE
        and w_out.shape == (chunks * TILE, chunks * TILE)
        and w_gate.shape[1] % TILE == 0
        and chunks * (w_gate.shape[1] // CAP) >= slots
    )


def local_fused(
    incoming, queries, new_kv, cache, lengths, slot_of, w_out, norm_gain, w_gate, w_up, w_down
):
    slots, requests = cache.shape[0], slot_of.shape[0]
    kv_local, groups = cache.shape[2] // (2 * HD), H // KVH
    width = incoming.shape[2]
    own_rows = requests // lax.axis_size("ffn")
    own_slots = lax.axis_index("att") * slots + jnp.arange(slots, dtype=jnp.int32)
    held = slot_of[None, :] == own_slots[:, None]
    holders = jnp.sum(jnp.where(held, jnp.arange(requests, dtype=jnp.int32)[None, :], 0), 1)
    q = queries.reshape(slots, STEPS, kv_local, groups, HD).transpose(0, 2, 1, 3, 4)
    kv = new_kv.reshape(slots, STEPS, kv_local, 2, HD).transpose(0, 2, 3, 1, 4)
    gathered_row = (slot_of // slots) * (slots * STEPS) + slot_of % slots
    gathered_row = gathered_row[:, None] + slots * jnp.arange(STEPS, dtype=jnp.int32)[None, :]
    place = (
        gathered_row.reshape(-1, 1) == jnp.arange(requests * STEPS, dtype=jnp.int32)[None, :]
    ).astype(jnp.bfloat16)
    mine = lax.dynamic_slice_in_dim(incoming, lax.axis_index("ffn") * own_rows, own_rows)
    own = fused(
        holders,
        lengths,
        q.reshape(slots, -1, HD),
        kv.reshape(slots, -1, HD),
        place,
        mine.reshape(own_rows * STEPS, width),
        norm_gain[None],
        cache,
        w_out,
        w_gate,
        w_up,
        w_down,
    )
    return own.reshape(own_rows, STEPS, width)


def local(
    incoming, queries, new_kv, cache, lengths, slot_of, w_out, norm_gain, w_gate, w_up, w_down
):
    if fits(queries, cache, w_out, w_gate, slot_of):
        return local_fused(
            incoming, queries, new_kv, cache, lengths, slot_of,
            w_out, norm_gain, w_gate, w_up, w_down,
        )
    ffn_count = lax.axis_size("ffn")
    att_index = lax.axis_index("att")
    ffn_index = lax.axis_index("ffn")
    request_count = slot_of.shape[0]
    slot_count = cache.shape[0]
    kv_local = cache.shape[2] // (2 * HD)
    groups = H // KVH
    score_scale = HD ** (-0.5)
    gathered_q, gathered_kv = (
        lax.all_gather(queries, "att", axis=0, tiled=True),
        lax.all_gather(new_kv, "att", axis=0, tiled=True),
    )
    holders = (
        jnp.zeros((request_count,), jnp.int32)
        .at[slot_of]
        .set(jnp.arange(request_count, dtype=jnp.int32))
    )
    my_requests = lax.dynamic_slice_in_dim(holders, att_index * slot_count, slot_count)
    query_mine = jnp.take(gathered_q, my_requests, axis=0).reshape(
        slot_count, STEPS, kv_local, groups, HD
    )
    fresh_mine = jnp.take(gathered_kv, my_requests, axis=0).reshape(
        slot_count, STEPS, kv_local, 2, HD
    )
    cache_view = cache.reshape(slot_count, CAP, kv_local, 2, HD)
    fresh_scores = (
        jnp.einsum(
            "rskgd,rtkd->rskgt",
            query_mine,
            fresh_mine[:, :, :, 0],
            preferred_element_type=jnp.float32,
        )
        * score_scale
    )
    causal = jnp.arange(STEPS)[None, :] <= jnp.arange(STEPS)[:, None]
    fresh_scores = jnp.where(causal[None, :, None, None, :], fresh_scores, -jnp.inf)
    kept_scores = (
        jnp.einsum(
            "rskgd,rckd->rskgc",
            query_mine,
            cache_view[:, :, :, 0],
            preferred_element_type=jnp.float32,
        )
        * score_scale
    )
    in_range = jnp.arange(CAP)[None, :] < lengths[:, None]
    kept_scores = jnp.where(in_range[:, None, None, None, :], kept_scores, -jnp.inf)
    top_score = jnp.maximum(jnp.max(kept_scores, -1), jnp.max(fresh_scores, -1))
    kept_exp = jnp.exp(kept_scores - top_score[..., None])
    fresh_exp = jnp.exp(fresh_scores - top_score[..., None])
    denominator = jnp.sum(kept_exp, -1) + jnp.sum(fresh_exp, -1)
    kept_prob = (kept_exp / denominator[..., None]).astype(jnp.bfloat16)
    fresh_prob = (fresh_exp / denominator[..., None]).astype(jnp.bfloat16)
    mixture = jnp.einsum(
        "rskgc,rckd->rskgd", kept_prob, cache_view[:, :, :, 1], preferred_element_type=jnp.float32
    )
    mixture = mixture + jnp.einsum(
        "rskgt,rtkd->rskgd", fresh_prob, fresh_mine[:, :, :, 1], preferred_element_type=jnp.float32
    )
    attended = mixture.astype(jnp.bfloat16).reshape(slot_count, STEPS, kv_local * groups * HD)
    shard_rows = lax.all_gather(attended, "att", axis=0, tiled=True)
    row_count = shard_rows.shape[0]
    flattened = shard_rows.reshape(row_count * STEPS, shard_rows.shape[2])
    heads_slots = jnp.dot(flattened, w_out, preferred_element_type=jnp.float32).reshape(
        row_count, STEPS, w_out.shape[1]
    )
    heads_requests = jnp.take(heads_slots, slot_of, axis=0)
    heads_total = lax.psum(heads_requests, "ffn")
    residual = (incoming.astype(jnp.float32) + heads_total).astype(jnp.bfloat16)
    residual_wide = residual.astype(jnp.float32)
    squares = lax.psum(jnp.sum(residual_wide * residual_wide, -1), "att")
    normed = (residual_wide * lax.rsqrt(squares / D + epsilon)[..., None] * norm_gain).astype(
        jnp.bfloat16
    )
    normed = normed.reshape(request_count * STEPS, normed.shape[2])
    gate_term = jnp.dot(normed, w_gate, preferred_element_type=jnp.float32)
    upward_term = jnp.dot(normed, w_up, preferred_element_type=jnp.float32)
    unit_share = lax.psum_scatter(
        jnp.concatenate([gate_term, upward_term], 1), "att", scatter_dimension=0, tiled=True
    )
    unit_width = w_gate.shape[1]
    hidden_share = (jax.nn.silu(unit_share[:, :unit_width]) * unit_share[:, unit_width:]).astype(
        jnp.bfloat16
    )
    down_part = jnp.dot(
        lax.all_gather(hidden_share, "att", axis=0, tiled=True),
        w_down,
        preferred_element_type=jnp.float32,
    )
    out_share = lax.psum_scatter(down_part, "ffn", scatter_dimension=0, tiled=True)
    row_share = request_count // ffn_count
    own_state = lax.dynamic_slice_in_dim(residual_wide, ffn_index * row_share, row_share, 0)
    return (own_state + out_share.reshape(row_share, STEPS, out_share.shape[1])).astype(
        jnp.bfloat16
    )


def solution(mesh):
    return jax.shard_map(
        local,
        mesh=mesh,
        in_specs=(
            P("parts", None, "att"),
            P(("parts", "att"), None, "ffn"),
            P(("parts", "att"), None, "ffn"),
            P(("parts", "att"), None, "ffn"),
            P(("parts", "att")),
            P("parts"),
            P("ffn", "att"),
            P("att"),
            P("att", "ffn"),
            P("att", "ffn"),
            P("ffn", "att"),
        ),
        out_specs=P(("parts", "ffn"), None, "att"),
        check_vma=False,
    )
```

```python
import functools

import jax
import jax.numpy as jnp
from jax import lax
from jax.experimental import pallas as pl
from jax.experimental.pallas import tpu as pltpu
from jax.sharding import PartitionSpec as P

D = 8192
H = 64
KVH = 8
HD = 128
STEPS = 2
CAP = 640


epsilon = 1e-05
TILE = 512
MESH = pl.DeviceIdType.MESH


def layer_kernel(
    cfg, holders, slots_row, lengths, q, kv, incoming, gain, cache, wo, wg, wu, wd, out,
    place, kept_in, gq, gkv, of, tb, attended,
    wo_v, wg_v, wu_v, wd_v,
    fa, pa, ra, sm, rm, om, res, h, ss, ssr,
    fg, s1, o1, r1, s2, o2, r2, hb,
    pd, od, rd,
    wo_s, wg_s, wu_s, wd_s,
    in_s, a_ss, a_rs, m_ss, m_rs, g_ss, g_rs, n_ss, n_rs, f_ss, f_rs, q_ss, q_rs,
    c1_ss, c1_rs, c2_ss, c2_rs,
    hp_ss, hp_rs, hx_ss, hx_rs, hf_ss, hf_rs,
    d_ss, d_rs,
    cache_s, qp_ss, qp_rs, qx_ss, qx_rs, qf_ss, qf_rs,
    tp_ss, tp_rs, tx_ss, tx_rs, tf_ss, tf_rs,
):
    Z, RB, T, NA, NF = cfg
    S = cache.shape[0]
    kv_local = cache.shape[2] // (2 * HD)
    groups = H // KVH
    QR = STEPS * groups
    per = wd_v.shape[1] // CAP
    A = 4
    z = lax.axis_index("ffn")
    a = lax.axis_index("att")
    x, c = a // 2, a % 2
    partner = 2 * x + (1 - c)
    xpeer = 2 * (1 - x) + c
    bf, f32 = jnp.bfloat16, jnp.float32

    def wcopy(src, dst, sem, k):
        return pltpu.make_async_copy(
            src.at[:, pl.ds(pl.multiple_of(k * T, T), T)], dst.at[k], sem.at[k]
        )

    def kept_rows(i):
        return pl.ds(pl.multiple_of((i % per) * CAP, CAP), CAP)

    def cache_copy(i):
        return pltpu.make_async_copy(cache.at[i], wd_v.at[i // per, kept_rows(i)], cache_s.at[i])

    @pl.loop(0, S)
    def _(i):
        cache_copy(i).start()

    half = z // 2
    in_copy = pltpu.make_async_copy(
        incoming.at[pl.ds(half * kept_in.shape[0], kept_in.shape[0])], kept_in, in_s.at[0]
    )
    in_copy.start()
    for k in range(NA):
        wcopy(wo, wo_v, wo_s, k).start()
    for k in range(NF):
        wcopy(wg, wg_v, wg_s, k).start()
        wcopy(wu, wu_v, wu_s, k).start()

    barrier = pltpu.get_barrier_semaphore()
    for d in range(1, Z):
        pl.semaphore_signal(barrier, 1, device_id={"ffn": (z + d) % Z}, device_id_type=MESH)
    for d in range(1, A):
        pl.semaphore_signal(barrier, 1, device_id={"att": (a + d) % A}, device_id_type=MESH)
    pl.semaphore_wait(barrier, Z - 1 + A - 1)

    def remote(src, dst, ss_, rs_, axis, peer):
        return pltpu.make_async_remote_copy(
            src_ref=src, dst_ref=dst, send_sem=ss_, recv_sem=rs_,
            device_id={axis: peer}, device_id_type=MESH,
        )

    inside = z * (Z - 1 - z)
    inner = 1 + half
    outer = 3 * (z - 1)
    other = 3 - z

    def half_of(ref, k, which):
        return ref.at[k, which]

    def a_copy(k, peer):
        return remote(pa.at[k], ra.at[k], a_ss.at[k], a_rs.at[k], "ffn", peer)

    def m_copy(k):
        return remote(sm.at[k], rm.at[k], m_ss.at[k], m_rs.at[k], "ffn", other)

    def g_copy(k, which):
        block = half_of(res, k, which)
        return remote(block, block, g_ss.at[k], g_rs.at[k], "ffn", other)

    def n_copy(k, which, peer):
        block = half_of(res, k, which)
        return remote(block, block, n_ss.at[k], n_rs.at[k], "ffn", peer)

    def f_copy(k, which, peer):
        block = half_of(res, k, which)
        return remote(block, block, f_ss.at[k], f_rs.at[k], "ffn", peer)

    def q_copy(d):
        peer = (a + d) % A
        return remote(ss.at[peer], ssr.at[d - 1], q_ss.at[d - 1], q_rs.at[d - 1], "att", peer)

    def c1_copy(k):
        return remote(s1.at[k], r1.at[k], c1_ss.at[k], c1_rs.at[k], "att", partner)

    def c2_copy(k):
        return remote(s2.at[k], r2.at[k], c2_ss.at[k], c2_rs.at[k], "att", xpeer)

    def hp_copy(k, block):
        return remote(hb.at[k, block], hb.at[k, block], hp_ss.at[k], hp_rs.at[k], "att", partner)

    def hx_copy(k, block):
        return remote(hb.at[k, block], hb.at[k, block], hx_ss.at[k], hx_rs.at[k], "att", xpeer)

    def hf_copy(k, block):
        return remote(hb.at[k, block], hb.at[k, block], hf_ss.at[k], hf_rs.at[k], "att", partner)

    def d_copy(k, d):
        peer = (z + d) % Z
        return remote(pd.at[k, peer], rd.at[k, d - 1], d_ss.at[k, d - 1], d_rs.at[k, d - 1], "ffn", peer)

    def block_of(ref, owner):
        return ref.at[pl.ds(owner * S, S)]

    for i, (mine, everyone) in enumerate(((q, gq), (kv, gkv))):
        remote(mine, block_of(everyone, a), qx_ss.at[i], qx_rs.at[i], "att", xpeer).start()
        remote(mine, block_of(everyone, a), qp_ss.at[i], qp_rs.at[i], "att", partner).start()
        everyone[pl.ds(a * S, S)] = mine[...]

    def qf_copy(i, everyone):
        block = block_of(everyone, xpeer)
        return remote(block, block, qf_ss.at[i], qf_rs.at[i], "att", partner)

    R = slots_row.shape[1]

    shift = S.bit_length() - 1
    spread_row = lax.broadcasted_iota(jnp.int32, (R, R * STEPS), 0) * STEPS
    spread_col = lax.broadcasted_iota(jnp.int32, (R, R * STEPS), 1)
    spread = (spread_col >= spread_row) & (spread_col < spread_row + STEPS)
    slot_at = jnp.dot(
        jnp.broadcast_to(slots_row[...].astype(f32), (8, R)).astype(bf),
        jnp.where(spread, 1.0, 0.0).astype(bf),
        preferred_element_type=f32,
    )[:1]
    row = lax.broadcasted_iota(jnp.int32, (R * STEPS, R * STEPS), 0)
    col = lax.broadcasted_iota(jnp.int32, (R * STEPS, R * STEPS), 1)
    row_slot = ((row >> (shift + 1)) << shift) + (row & (S - 1))
    row_step = (row >> shift) & (STEPS - 1)
    chosen = (row_slot.astype(f32) == slot_at) & (row_step == (col & (STEPS - 1)))
    place[...] = jnp.where(chosen, 1.0, 0.0).astype(bf)

    far = 2 * (1 - x) + (1 - c)
    for i, (mine, everyone) in enumerate(((q, gq), (kv, gkv))):
        remote(mine, block_of(everyone, xpeer), qx_ss.at[i], qx_rs.at[i], "att", xpeer).wait_recv()
        qf_copy(i, everyone).start()
    for i, (mine, everyone) in enumerate(((q, gq), (kv, gkv))):
        remote(mine, block_of(everyone, partner), qp_ss.at[i], qp_rs.at[i], "att", partner).wait_recv()
        block = block_of(everyone, far)
        remote(block, block, qf_ss.at[i], qf_rs.at[i], "att", partner).wait_recv()

    def attend(i, g):
        holder, length = holders[i], lengths[i]
        rows = gq[holder][g * QR:(g + 1) * QR]
        fresh = gkv[holder].astype(f32)
        kept = kept_rows(i)
        keys = wd_v[i // per, kept, g * 2 * HD:(g * 2 + 1) * HD]
        values = wd_v[i // per, kept, (g * 2 + 1) * HD:(g * 2 + 2) * HD]
        scale = HD ** (-0.5)
        scores = lax.dot_general(
            rows, keys, (((1,), (1,)), ((), ())), preferred_element_type=f32
        ) * scale
        column = lax.broadcasted_iota(jnp.int32, scores.shape, 1)
        scores = jnp.where(column < length, scores, -jnp.inf)
        wide = rows.astype(f32)
        step = lax.broadcasted_iota(jnp.int32, (QR, 1), 0) // groups
        new_scores = []
        for t in range(STEPS):
            at = g * 2 * STEPS + t
            score = jnp.sum(wide * fresh[at:at + 1], -1, keepdims=True) * scale
            new_scores.append(jnp.where(step >= t, score, -jnp.inf))
        top = jnp.max(scores, -1, keepdims=True)
        for score in new_scores:
            top = jnp.maximum(top, score)
        weights = jnp.exp(scores - top)
        total = jnp.sum(weights, -1, keepdims=True)
        new_weights = [jnp.exp(score - top) for score in new_scores]
        for weight in new_weights:
            total = total + weight
        mixed = jnp.dot((weights / total).astype(bf), values, preferred_element_type=f32)
        for t in range(STEPS):
            at = g * 2 * STEPS + STEPS + t
            mixed = mixed + (new_weights[t] / total).astype(bf).astype(f32) * fresh[at:at + 1]
        of[pl.ds(pl.multiple_of(i * QR, QR), QR), :] = mixed

    def t_copy(k, ss_, rs_, block, peer):
        return remote(tb.at[k, block], tb.at[k, block], ss_.at[k], rs_.at[k], "att", peer)

    heads = T // HD
    chunks = groups // heads
    for g in range(kv_local):
        @pl.loop(0, S // 4)
        def _(j):
            for n in range(4):
                if g == 0:
                    cache_copy(j * 4 + n).wait()
            for n in range(4):
                attend(j * 4 + n, g)

        for k in range(chunks):
            for t in range(STEPS):
                for n in range(heads):
                    row = t * groups + k * heads + n
                    tb[g * chunks + k, a, t * S:(t + 1) * S, n * HD:(n + 1) * HD] = of[
                        pl.ds(row, S, stride=QR), :
                    ].astype(bf)
            t_copy(g * chunks + k, tx_ss, tx_rs, a, xpeer).start()
            t_copy(g * chunks + k, tp_ss, tp_rs, a, partner).start()

    for k in range(NA):
        wcopy(wd, wd_v, wd_s, k).start()
    for k in range(NA):
        t_copy(k, tx_ss, tx_rs, xpeer, xpeer).wait_recv()
        t_copy(k, tf_ss, tf_rs, xpeer, partner).start()
    for k in range(NA):
        t_copy(k, tp_ss, tp_rs, partner, partner).wait_recv()
        t_copy(k, tf_ss, tf_rs, far, partner).wait_recv()
        attended[:, k * T:(k + 1) * T] = lax.dot_general(
            place[...], tb[k].reshape(Z * RB, T), (((0,), (0,)), ((), ())),
            preferred_element_type=f32,
        ).astype(bf)

    in_copy.wait()

    def own_half(k):
        m_copy(k).wait_recv()
        kept = kept_in[:, :, k * T:(k + 1) * T].astype(f32).reshape(2, RB, T)
        res[k, half] = (kept + om[k] + rm[k].astype(f32)).astype(bf)
        g_copy(k, half).start()
        n_copy(k, half, outer).start()

    def pass_on(k):
        g_copy(k, 1 - half).wait_recv()
        f_copy(k, 1 - half, outer).start()

    for k in range(NA):
        wcopy(wo, wo_v, wo_s, k).wait()
        fa[...] = jnp.dot(attended[...], wo_v[k], preferred_element_type=f32).reshape(fa.shape)

        @pl.when(inside == 0)
        def _():
            pa[k] = fa[...].astype(bf)
            a_copy(k, inner).start()

        @pl.when(inside > 0)
        def _():
            a_copy(k, outer).wait_recv()
            theirs = 1 - half
            sm[k] = (fa[theirs] + ra[k, theirs].astype(f32)).astype(bf)
            m_copy(k).start()
            om[k] = fa[half] + ra[k, half].astype(f32)
            if k > 0:
                own_half(k - 1)
            if k > 1:
                pass_on(k - 2)

    @pl.when(inside > 0)
    def _():
        own_half(NA - 1)
        for k in range(max(NA - 2, 0), NA):
            pass_on(k)

    squares = jnp.zeros((Z, RB, 1), f32)
    for k in range(NA):
        @pl.when(inside == 0)
        def _():
            n_copy(k, half, inner).wait_recv()
            f_copy(k, 1 - half, inner).wait_recv()

        wide = res[k].astype(f32).reshape(Z, RB, T)
        squares = squares + jnp.sum(wide * wide, -1, keepdims=True)
        h[:, k * T:(k + 1) * T] = (
            (wide * gain[:, k * T:(k + 1) * T]).astype(bf).reshape(Z * RB, T)
        )
    ss[...] = jnp.broadcast_to(squares.reshape(A, ss.shape[1], 1), ss.shape)
    for d in range(1, A):
        q_copy(d).start()

    def first(k):
        wcopy(wg, wg_v, wg_s, k).wait()
        wcopy(wu, wu_v, wu_s, k).wait()
        for i, w in enumerate((wg_v, wu_v)):
            p = jnp.dot(h[...], w[k], preferred_element_type=f32)
            fg[i] = p.reshape(fg.shape[1:])
            for xx in range(2):
                s1[k, i, xx] = fg[i, 2 * xx + (1 - c)].astype(bf)
                o1[k % 2, i, xx] = fg[i, 2 * xx + c]
        c1_copy(k).start()

    def second(k):
        c1_copy(k).wait_recv()
        for i in range(2):
            s2[k, i] = (o1[k % 2, i, 1 - x] + r1[k, i, 1 - x].astype(f32)).astype(bf)
            o2[k, i] = o1[k % 2, i, x] + r1[k, i, x].astype(f32)
        c2_copy(k).start()

    first(0)

    @pl.loop(1, NF)
    def _(k):
        first(k)
        second(k - 1)

    second(NF - 1)

    total_squares = ss[a]
    for d in range(1, A):
        q_copy(d).wait_recv()
        total_squares = total_squares + ssr[d - 1]
    inverse = lax.rsqrt(total_squares / D + epsilon)[:, :1]

    @pl.loop(0, NF)
    def _(k):
        c2_copy(k).wait_recv()
        gate = (o2[k, 0] + r2[k, 0].astype(f32)) * inverse
        up = (o2[k, 1] + r2[k, 1].astype(f32)) * inverse
        hb[k, a] = (gate / (1.0 + jnp.exp(-gate)) * up).astype(bf)
        hx_copy(k, a).start()
        hp_copy(k, a).start()

    @pl.loop(0, NF)
    def _(k):
        hx_copy(k, xpeer).wait_recv()
        hf_copy(k, xpeer).start()

    @pl.loop(0, NF)
    def _(k):
        hp_copy(k, partner).wait_recv()
        hf_copy(k, 2 * (1 - x) + (1 - c)).wait_recv()

    @pl.loop(0, NA)
    def _(n):
        wcopy(wd, wd_v, wd_s, n).wait()
        p = jnp.zeros((Z * RB, T), f32)
        for k in range(NF):
            p = p + jnp.dot(
                hb[k].reshape(Z * RB, T), wd_v[n, k * T:(k + 1) * T, :], preferred_element_type=f32
            )
        p = p.reshape(Z, RB, T)
        fa[...] = p.reshape(fa.shape)
        pd[n] = p.astype(bf)
        od[n] = fa[half, z % 2]
        for d in range(1, Z):
            d_copy(n, d).start()

    for n in range(NA):
        total = res[n, half, z % 2].astype(f32) + od[n]
        for d in range(1, Z):
            d_copy(n, d).wait_recv()
            total = total + rd[n, d - 1].astype(f32)
        out[:, :, n * T:(n + 1) * T] = total.reshape(out.shape[0], STEPS, T).astype(bf)

    for k in range(NA):
        for d in range(1, Z):
            d_copy(k, d).wait_send()

    @pl.when(inside == 0)
    def _():
        for k in range(NA):
            a_copy(k, inner).wait_send()

    @pl.when(inside > 0)
    def _():
        for k in range(NA):
            m_copy(k).wait_send()
            g_copy(k, half).wait_send()
            n_copy(k, half, outer).wait_send()
            f_copy(k, 1 - half, outer).wait_send()

    for d in range(1, A):
        q_copy(d).wait_send()
    for i, (mine, everyone) in enumerate(((q, gq), (kv, gkv))):
        remote(mine, block_of(everyone, a), qx_ss.at[i], qx_rs.at[i], "att", xpeer).wait_send()
        remote(mine, block_of(everyone, a), qp_ss.at[i], qp_rs.at[i], "att", partner).wait_send()
        qf_copy(i, everyone).wait_send()
    for k in range(NA):
        t_copy(k, tx_ss, tx_rs, a, xpeer).wait_send()
        t_copy(k, tp_ss, tp_rs, a, partner).wait_send()
        t_copy(k, tf_ss, tf_rs, xpeer, partner).wait_send()
    for k in range(NF):
        c1_copy(k).wait_send()
        c2_copy(k).wait_send()
        hp_copy(k, a).wait_send()
        hx_copy(k, a).wait_send()
        hf_copy(k, xpeer).wait_send()


def fused(holders, slots, lengths, q, kv, incoming, gain, cache, w_out, w_gate, w_up, w_down):
    Z = lax.axis_size("ffn")
    rows, kdim = slots.shape[0] * STEPS, w_out.shape[0]
    width = w_out.shape[1]
    units = w_gate.shape[1]
    RB, T = rows // Z, TILE
    NA, NF = width // T, units // T
    AB = rows // 4
    S = cache.shape[0]
    bf, f32 = jnp.bfloat16, jnp.float32
    V = pltpu.VMEM
    dma = pltpu.SemaphoreType.DMA
    vm = pl.BlockSpec(memory_space=pltpu.VMEM)
    sm = pl.BlockSpec(memory_space=pltpu.SMEM)
    hbm = pl.BlockSpec(memory_space=pl.ANY)
    scratch = [
        V((rows, rows), bf), V((incoming.shape[0] // 2,) + incoming.shape[1:], bf),
        V((4 * S,) + q.shape[1:], bf), V((4 * S,) + kv.shape[1:], bf),
        V((S * STEPS * (H // KVH), HD), f32), V((kdim // T, 4, AB, T), bf), V((rows, kdim), bf),
        V((NA, kdim, T), bf), V((NF, width, T), bf), V((NF, width, T), bf), V((NA, units, T), bf),
        V((2, 2, RB, T), f32), V((NA, 2, 2, RB, T), bf), V((NA, 2, 2, RB, T), bf), V((NA, 2, RB, T), bf),
        V((NA, 2, RB, T), bf), V((NA, 2, RB, T), f32),
        V((NA, 2, 2, RB, T), bf), V((rows, width), bf), V((4, AB, 128), f32), V((3, AB, 128), f32),
        V((2, 4, AB, T), f32), V((NF, 2, 2, AB, T), bf), V((2, 2, 2, AB, T), f32),
        V((NF, 2, 2, AB, T), bf), V((NF, 2, AB, T), bf), V((NF, 2, AB, T), f32),
        V((NF, 2, AB, T), bf), V((NF, 4, AB, T), bf),
        V((NA, Z, RB, T), bf), V((NA, RB, T), f32), V((NA, Z - 1, RB, T), bf),
        dma((NA,)), dma((NF,)), dma((NF,)), dma((NA,)),
        dma((1,)),
    ] + [dma((NA,)) for _ in range(10)] + [dma((3,)), dma((3,))]
    scratch += [dma((NF,)) for _ in range(10)] + [dma((NA, Z - 1)), dma((NA, Z - 1))]
    scratch += [dma((S,))] + [dma((2,)) for _ in range(6)] + [dma((NA,)) for _ in range(6)]
    return pl.pallas_call(
        functools.partial(layer_kernel, (Z, RB, T, NA, NF)),
        out_shape=jax.ShapeDtypeStruct((RB // STEPS, STEPS, width), bf),
        in_specs=[sm, vm, sm, vm, vm, hbm, vm, hbm, hbm, hbm, hbm, hbm],
        out_specs=vm,
        scratch_shapes=scratch,
        compiler_params=pltpu.CompilerParams(
            collective_id=1, has_side_effects=True, vmem_limit_bytes=67043328
        ),
    )(holders, slots[None], lengths, q, kv, incoming, gain, cache, w_out, w_gate, w_up, w_down)


def fits(queries, cache, w_out, w_gate, slot_of):
    slots = cache.shape[0]
    chunks = w_out.shape[1] // TILE
    return (
        lax.axis_size("att") == 4
        and lax.axis_size("ffn") == 4
        and slots % 16 == 0
        and slots & (slots - 1) == 0
        and slot_of.shape[0] == 4 * slots
        and slot_of.shape[0] * STEPS <= 128
        and cache.shape[2] == TILE
        and w_out.shape == (chunks * TILE, chunks * TILE)
        and w_gate.shape[1] % TILE == 0
        and chunks * (w_gate.shape[1] // CAP) >= slots
    )


def local_fused(
    incoming, queries, new_kv, cache, lengths, slot_of, w_out, norm_gain, w_gate, w_up, w_down
):
    slots = cache.shape[0]
    kv_local, groups = cache.shape[2] // (2 * HD), H // KVH
    q = queries.reshape(slots, STEPS, kv_local, groups, HD).transpose(0, 2, 1, 3, 4)
    kv = new_kv.reshape(slots, STEPS, kv_local, 2, HD).transpose(0, 2, 3, 1, 4)
    requests = jnp.arange(slot_of.shape[0], dtype=jnp.int32)
    own_slots = lax.axis_index("att") * slots + jnp.arange(slots, dtype=jnp.int32)
    held = slot_of[None, :] == own_slots[:, None]
    return fused(
        jnp.sum(jnp.where(held, requests[None, :], 0), 1),
        slot_of,
        lengths,
        q.reshape(slots, -1, HD),
        kv.reshape(slots, -1, HD),
        incoming,
        norm_gain[None],
        cache,
        w_out,
        w_gate,
        w_up,
        w_down,
    )


def local(
    incoming, queries, new_kv, cache, lengths, slot_of, w_out, norm_gain, w_gate, w_up, w_down
):
    if fits(queries, cache, w_out, w_gate, slot_of):
        return local_fused(
            incoming, queries, new_kv, cache, lengths, slot_of,
            w_out, norm_gain, w_gate, w_up, w_down,
        )
    ffn_count = lax.axis_size("ffn")
    att_index = lax.axis_index("att")
    ffn_index = lax.axis_index("ffn")
    request_count = slot_of.shape[0]
    slot_count = cache.shape[0]
    kv_local = cache.shape[2] // (2 * HD)
    groups = H // KVH
    score_scale = HD ** (-0.5)
    gathered_q, gathered_kv = (
        lax.all_gather(queries, "att", axis=0, tiled=True),
        lax.all_gather(new_kv, "att", axis=0, tiled=True),
    )
    holders = (
        jnp.zeros((request_count,), jnp.int32)
        .at[slot_of]
        .set(jnp.arange(request_count, dtype=jnp.int32))
    )
    my_requests = lax.dynamic_slice_in_dim(holders, att_index * slot_count, slot_count)
    query_mine = jnp.take(gathered_q, my_requests, axis=0).reshape(
        slot_count, STEPS, kv_local, groups, HD
    )
    fresh_mine = jnp.take(gathered_kv, my_requests, axis=0).reshape(
        slot_count, STEPS, kv_local, 2, HD
    )
    cache_view = cache.reshape(slot_count, CAP, kv_local, 2, HD)
    fresh_scores = (
        jnp.einsum(
            "rskgd,rtkd->rskgt",
            query_mine,
            fresh_mine[:, :, :, 0],
            preferred_element_type=jnp.float32,
        )
        * score_scale
    )
    causal = jnp.arange(STEPS)[None, :] <= jnp.arange(STEPS)[:, None]
    fresh_scores = jnp.where(causal[None, :, None, None, :], fresh_scores, -jnp.inf)
    kept_scores = (
        jnp.einsum(
            "rskgd,rckd->rskgc",
            query_mine,
            cache_view[:, :, :, 0],
            preferred_element_type=jnp.float32,
        )
        * score_scale
    )
    in_range = jnp.arange(CAP)[None, :] < lengths[:, None]
    kept_scores = jnp.where(in_range[:, None, None, None, :], kept_scores, -jnp.inf)
    top_score = jnp.maximum(jnp.max(kept_scores, -1), jnp.max(fresh_scores, -1))
    kept_exp = jnp.exp(kept_scores - top_score[..., None])
    fresh_exp = jnp.exp(fresh_scores - top_score[..., None])
    denominator = jnp.sum(kept_exp, -1) + jnp.sum(fresh_exp, -1)
    kept_prob = (kept_exp / denominator[..., None]).astype(jnp.bfloat16)
    fresh_prob = (fresh_exp / denominator[..., None]).astype(jnp.bfloat16)
    mixture = jnp.einsum(
        "rskgc,rckd->rskgd", kept_prob, cache_view[:, :, :, 1], preferred_element_type=jnp.float32
    )
    mixture = mixture + jnp.einsum(
        "rskgt,rtkd->rskgd", fresh_prob, fresh_mine[:, :, :, 1], preferred_element_type=jnp.float32
    )
    attended = mixture.astype(jnp.bfloat16).reshape(slot_count, STEPS, kv_local * groups * HD)
    shard_rows = lax.all_gather(attended, "att", axis=0, tiled=True)
    row_count = shard_rows.shape[0]
    flattened = shard_rows.reshape(row_count * STEPS, shard_rows.shape[2])
    heads_slots = jnp.dot(flattened, w_out, preferred_element_type=jnp.float32).reshape(
        row_count, STEPS, w_out.shape[1]
    )
    heads_requests = jnp.take(heads_slots, slot_of, axis=0)
    heads_total = lax.psum(heads_requests, "ffn")
    residual = (incoming.astype(jnp.float32) + heads_total).astype(jnp.bfloat16)
    residual_wide = residual.astype(jnp.float32)
    squares = lax.psum(jnp.sum(residual_wide * residual_wide, -1), "att")
    normed = (residual_wide * lax.rsqrt(squares / D + epsilon)[..., None] * norm_gain).astype(
        jnp.bfloat16
    )
    normed = normed.reshape(request_count * STEPS, normed.shape[2])
    gate_term = jnp.dot(normed, w_gate, preferred_element_type=jnp.float32)
    upward_term = jnp.dot(normed, w_up, preferred_element_type=jnp.float32)
    unit_share = lax.psum_scatter(
        jnp.concatenate([gate_term, upward_term], 1), "att", scatter_dimension=0, tiled=True
    )
    unit_width = w_gate.shape[1]
    hidden_share = (jax.nn.silu(unit_share[:, :unit_width]) * unit_share[:, unit_width:]).astype(
        jnp.bfloat16
    )
    down_part = jnp.dot(
        lax.all_gather(hidden_share, "att", axis=0, tiled=True),
        w_down,
        preferred_element_type=jnp.float32,
    )
    out_share = lax.psum_scatter(down_part, "ffn", scatter_dimension=0, tiled=True)
    row_share = request_count // ffn_count
    own_state = lax.dynamic_slice_in_dim(residual_wide, ffn_index * row_share, row_share, 0)
    return (own_state + out_share.reshape(row_share, STEPS, out_share.shape[1])).astype(
        jnp.bfloat16
    )


def solution(mesh):
    return jax.shard_map(
        local,
        mesh=mesh,
        in_specs=(
            P("parts", None, "att"),
            P(("parts", "att"), None, "ffn"),
            P(("parts", "att"), None, "ffn"),
            P(("parts", "att"), None, "ffn"),
            P(("parts", "att")),
            P("parts"),
            P("ffn", "att"),
            P("att"),
            P("att", "ffn"),
            P("att", "ffn"),
            P("ffn", "att"),
        ),
        out_specs=P(("parts", "ffn"), None, "att"),
        check_vma=False,
    )
```

```python
import functools

import jax
import jax.numpy as jnp
from jax import lax
from jax.experimental import pallas as pl
from jax.experimental.pallas import tpu as pltpu
from jax.sharding import PartitionSpec as P

D = 8192
H = 64
KVH = 8
HD = 128
STEPS = 2
CAP = 640


epsilon = 1e-05
TILE = 512
LAG = 3
MESH = pl.DeviceIdType.MESH


def layer_kernel(
    cfg, holders, slots_row, lengths, q, kv, incoming, gain, cache, wo, wg, wu, wd, out,
    place, kept_in, gq, gkv, of, tb, attended,
    wo_v, wg_v, wu_v, wd_v,
    fa, pa, ra, sm, rm, om, res, h, ss, ssr,
    fg, s1, o1, r1, s2, o2, r2, hb,
    pd, od, rd,
    wo_s, wg_s, wu_s, wd_s,
    in_s, a_ss, a_rs, m_ss, m_rs, g_ss, g_rs, n_ss, n_rs, f_ss, f_rs, q_ss, q_rs,
    c1_ss, c1_rs, c2_ss, c2_rs,
    hp_ss, hp_rs, hx_ss, hx_rs, hf_ss, hf_rs,
    d_ss, d_rs,
    cache_s, qp_ss, qp_rs, qx_ss, qx_rs, qf_ss, qf_rs,
    tp_ss, tp_rs, tx_ss, tx_rs, tf_ss, tf_rs,
):
    Z, RB, T, NA, NF = cfg
    S = cache.shape[0]
    kv_local = cache.shape[2] // (2 * HD)
    groups = H // KVH
    QR = STEPS * groups
    per = wd_v.shape[1] // CAP
    A = 4
    z = lax.axis_index("ffn")
    a = lax.axis_index("att")
    x, c = a // 2, a % 2
    partner = 2 * x + (1 - c)
    xpeer = 2 * (1 - x) + c
    bf, f32 = jnp.bfloat16, jnp.float32

    def wcopy(src, dst, sem, k):
        return pltpu.make_async_copy(
            src.at[:, pl.ds(pl.multiple_of(k * T, T), T)], dst.at[k], sem.at[k]
        )

    def kept_rows(i):
        return pl.ds(pl.multiple_of((i % per) * CAP, CAP), CAP)

    def cache_copy(i):
        return pltpu.make_async_copy(cache.at[i], wd_v.at[i // per, kept_rows(i)], cache_s.at[i])

    @pl.loop(0, S)
    def _(i):
        cache_copy(i).start()

    half = z // 2
    in_copy = pltpu.make_async_copy(
        incoming.at[pl.ds(half * kept_in.shape[0], kept_in.shape[0])], kept_in, in_s.at[0]
    )
    in_copy.start()
    for k in range(NA):
        wcopy(wo, wo_v, wo_s, k).start()
    for k in range(NF):
        wcopy(wg, wg_v, wg_s, k).start()
        wcopy(wu, wu_v, wu_s, k).start()

    barrier = pltpu.get_barrier_semaphore()
    for d in range(1, Z):
        pl.semaphore_signal(barrier, 1, device_id={"ffn": (z + d) % Z}, device_id_type=MESH)
    for d in range(1, A):
        pl.semaphore_signal(barrier, 1, device_id={"att": (a + d) % A}, device_id_type=MESH)
    pl.semaphore_wait(barrier, Z - 1 + A - 1)

    def remote(src, dst, ss_, rs_, axis, peer):
        return pltpu.make_async_remote_copy(
            src_ref=src, dst_ref=dst, send_sem=ss_, recv_sem=rs_,
            device_id={axis: peer}, device_id_type=MESH,
        )

    inside = z * (Z - 1 - z)
    inner = 1 + half
    outer = 3 * (z - 1)
    other = 3 - z

    def half_of(ref, k, which):
        return ref.at[k, which]

    def a_copy(k, peer):
        return remote(pa.at[k], ra.at[k], a_ss.at[k], a_rs.at[k], "ffn", peer)

    def m_copy(k):
        return remote(sm.at[k], rm.at[k], m_ss.at[k], m_rs.at[k], "ffn", other)

    def g_copy(k, which):
        block = half_of(res, k, which)
        return remote(block, block, g_ss.at[k], g_rs.at[k], "ffn", other)

    def n_copy(k, which, peer):
        block = half_of(res, k, which)
        return remote(block, block, n_ss.at[k], n_rs.at[k], "ffn", peer)

    def f_copy(k, which, peer):
        block = half_of(res, k, which)
        return remote(block, block, f_ss.at[k], f_rs.at[k], "ffn", peer)

    def q_copy(d):
        peer = (a + d) % A
        return remote(ss.at[peer], ssr.at[d - 1], q_ss.at[d - 1], q_rs.at[d - 1], "att", peer)

    def c1_copy(k):
        return remote(s1.at[k], r1.at[k], c1_ss.at[k], c1_rs.at[k], "att", partner)

    def c2_copy(k):
        return remote(s2.at[k], r2.at[k], c2_ss.at[k], c2_rs.at[k], "att", xpeer)

    def hp_copy(k, block):
        return remote(hb.at[k, block], hb.at[k, block], hp_ss.at[k], hp_rs.at[k], "att", partner)

    def hx_copy(k, block):
        return remote(hb.at[k, block], hb.at[k, block], hx_ss.at[k], hx_rs.at[k], "att", xpeer)

    def hf_copy(k, block):
        return remote(hb.at[k, block], hb.at[k, block], hf_ss.at[k], hf_rs.at[k], "att", partner)

    def d_copy(k, d):
        peer = (z + d) % Z
        return remote(pd.at[k, peer], rd.at[k, d - 1], d_ss.at[k, d - 1], d_rs.at[k, d - 1], "ffn", peer)

    def block_of(ref, owner):
        return ref.at[pl.ds(owner * S, S)]

    for i, (mine, everyone) in enumerate(((q, gq), (kv, gkv))):
        remote(mine, block_of(everyone, a), qx_ss.at[i], qx_rs.at[i], "att", xpeer).start()
        remote(mine, block_of(everyone, a), qp_ss.at[i], qp_rs.at[i], "att", partner).start()
        everyone[pl.ds(a * S, S)] = mine[...]

    def qf_copy(i, everyone):
        block = block_of(everyone, xpeer)
        return remote(block, block, qf_ss.at[i], qf_rs.at[i], "att", partner)

    R = slots_row.shape[1]

    shift = S.bit_length() - 1
    spread_row = lax.broadcasted_iota(jnp.int32, (R, R * STEPS), 0) * STEPS
    spread_col = lax.broadcasted_iota(jnp.int32, (R, R * STEPS), 1)
    spread = (spread_col >= spread_row) & (spread_col < spread_row + STEPS)
    slot_at = jnp.dot(
        jnp.broadcast_to(slots_row[...].astype(f32), (8, R)).astype(bf),
        jnp.where(spread, 1.0, 0.0).astype(bf),
        preferred_element_type=f32,
    )[:1]
    row = lax.broadcasted_iota(jnp.int32, (R * STEPS, R * STEPS), 0)
    col = lax.broadcasted_iota(jnp.int32, (R * STEPS, R * STEPS), 1)
    row_slot = ((row >> (shift + 1)) << shift) + (row & (S - 1))
    row_step = (row >> shift) & (STEPS - 1)
    chosen = (row_slot.astype(f32) == slot_at) & (row_step == (col & (STEPS - 1)))
    place[...] = jnp.where(chosen, 1.0, 0.0).astype(bf)

    far = 2 * (1 - x) + (1 - c)
    for i, (mine, everyone) in enumerate(((q, gq), (kv, gkv))):
        remote(mine, block_of(everyone, xpeer), qx_ss.at[i], qx_rs.at[i], "att", xpeer).wait_recv()
        qf_copy(i, everyone).start()
    for i, (mine, everyone) in enumerate(((q, gq), (kv, gkv))):
        remote(mine, block_of(everyone, partner), qp_ss.at[i], qp_rs.at[i], "att", partner).wait_recv()
        block = block_of(everyone, far)
        remote(block, block, qf_ss.at[i], qf_rs.at[i], "att", partner).wait_recv()

    def attend(i, g):
        holder, length = holders[i], lengths[i]
        rows = gq[holder][g * QR:(g + 1) * QR]
        fresh = gkv[holder].astype(f32)
        kept = kept_rows(i)
        keys = wd_v[i // per, kept, g * 2 * HD:(g * 2 + 1) * HD]
        values = wd_v[i // per, kept, (g * 2 + 1) * HD:(g * 2 + 2) * HD]
        scale = HD ** (-0.5)
        scores = lax.dot_general(
            rows, keys, (((1,), (1,)), ((), ())), preferred_element_type=f32
        ) * scale
        column = lax.broadcasted_iota(jnp.int32, scores.shape, 1)
        scores = jnp.where(column < length, scores, -jnp.inf)
        wide = rows.astype(f32)
        step = lax.broadcasted_iota(jnp.int32, (QR, 1), 0) // groups
        new_scores = []
        for t in range(STEPS):
            at = g * 2 * STEPS + t
            score = jnp.sum(wide * fresh[at:at + 1], -1, keepdims=True) * scale
            new_scores.append(jnp.where(step >= t, score, -jnp.inf))
        top = jnp.max(scores, -1, keepdims=True)
        for score in new_scores:
            top = jnp.maximum(top, score)
        weights = jnp.exp(scores - top)
        total = jnp.sum(weights, -1, keepdims=True)
        new_weights = [jnp.exp(score - top) for score in new_scores]
        for weight in new_weights:
            total = total + weight
        mixed = jnp.dot((weights / total).astype(bf), values, preferred_element_type=f32)
        for t in range(STEPS):
            at = g * 2 * STEPS + STEPS + t
            mixed = mixed + (new_weights[t] / total).astype(bf).astype(f32) * fresh[at:at + 1]
        of[pl.ds(pl.multiple_of(i * QR, QR), QR), :] = mixed

    def t_copy(k, ss_, rs_, block, peer):
        return remote(tb.at[k, block], tb.at[k, block], ss_.at[k], rs_.at[k], "att", peer)

    heads = T // HD
    chunks = groups // heads
    for g in range(kv_local):
        @pl.loop(0, S // 4)
        def _(j):
            for n in range(4):
                if g == 0:
                    cache_copy(j * 4 + n).wait()
            for n in range(4):
                attend(j * 4 + n, g)

        for k in range(chunks):
            for t in range(STEPS):
                for n in range(heads):
                    row = t * groups + k * heads + n
                    tb[g * chunks + k, a, t * S:(t + 1) * S, n * HD:(n + 1) * HD] = of[
                        pl.ds(row, S, stride=QR), :
                    ].astype(bf)
            t_copy(g * chunks + k, tx_ss, tx_rs, a, xpeer).start()
            t_copy(g * chunks + k, tp_ss, tp_rs, a, partner).start()

    for k in range(NA):
        wcopy(wd, wd_v, wd_s, k).start()
    for k in range(NA):
        t_copy(k, tx_ss, tx_rs, xpeer, xpeer).wait_recv()
        t_copy(k, tf_ss, tf_rs, xpeer, partner).start()
    for k in range(NA):
        t_copy(k, tp_ss, tp_rs, partner, partner).wait_recv()
        t_copy(k, tf_ss, tf_rs, far, partner).wait_recv()
        attended[:, k * T:(k + 1) * T] = lax.dot_general(
            place[...], tb[k].reshape(Z * RB, T), (((0,), (0,)), ((), ())),
            preferred_element_type=f32,
        ).astype(bf)

    in_copy.wait()

    def own_half(k):
        m_copy(k).wait_recv()
        kept = kept_in[:, :, k * T:(k + 1) * T].astype(f32).reshape(2, RB, T)
        res[k, half] = (kept + om[k] + rm[k].astype(f32)).astype(bf)
        g_copy(k, half).start()
        n_copy(k, half, outer).start()

    def pass_on(k):
        g_copy(k, 1 - half).wait_recv()
        f_copy(k, 1 - half, outer).start()

    for k in range(NA):
        wcopy(wo, wo_v, wo_s, k).wait()
        fa[...] = jnp.dot(attended[...], wo_v[k], preferred_element_type=f32).reshape(fa.shape)

        @pl.when(inside == 0)
        def _():
            pa[k] = fa[...].astype(bf)
            a_copy(k, inner).start()

        @pl.when(inside > 0)
        def _():
            a_copy(k, outer).wait_recv()
            theirs = 1 - half
            sm[k] = (fa[theirs] + ra[k, theirs].astype(f32)).astype(bf)
            m_copy(k).start()
            om[k] = fa[half] + ra[k, half].astype(f32)
            if k > 0:
                own_half(k - 1)
            if k > 1:
                pass_on(k - 2)

    @pl.when(inside > 0)
    def _():
        own_half(NA - 1)
        for k in range(max(NA - 2, 0), NA):
            pass_on(k)

    squares = jnp.zeros((Z, RB, 1), f32)
    for k in range(NA):
        @pl.when(inside == 0)
        def _():
            n_copy(k, half, inner).wait_recv()
            f_copy(k, 1 - half, inner).wait_recv()

        wide = res[k].astype(f32).reshape(Z, RB, T)
        squares = squares + jnp.sum(wide * wide, -1, keepdims=True)
        h[:, k * T:(k + 1) * T] = (
            (wide * gain[:, k * T:(k + 1) * T]).astype(bf).reshape(Z * RB, T)
        )
    ss[...] = jnp.broadcast_to(squares.reshape(A, ss.shape[1], 1), ss.shape)
    for d in range(1, A):
        q_copy(d).start()

    def first(k):
        wcopy(wg, wg_v, wg_s, k).wait()
        wcopy(wu, wu_v, wu_s, k).wait()
        for i, w in enumerate((wg_v, wu_v)):
            p = jnp.dot(h[...], w[k], preferred_element_type=f32)
            fg[i] = p.reshape(fg.shape[1:])
            for xx in range(2):
                s1[k, i, xx] = fg[i, 2 * xx + (1 - c)].astype(bf)
                o1[k % 2, i, xx] = fg[i, 2 * xx + c]
        c1_copy(k).start()

    def second(k):
        c1_copy(k).wait_recv()
        for i in range(2):
            s2[k, i] = (o1[k % 2, i, 1 - x] + r1[k, i, 1 - x].astype(f32)).astype(bf)
            o2[k, i] = o1[k % 2, i, x] + r1[k, i, x].astype(f32)
        c2_copy(k).start()

    def hidden(k, inverse):
        c2_copy(k).wait_recv()
        gate = (o2[k, 0] + r2[k, 0].astype(f32)) * inverse
        up = (o2[k, 1] + r2[k, 1].astype(f32)) * inverse
        hb[k, a] = (gate / (1.0 + jnp.exp(-gate)) * up).astype(bf)
        hx_copy(k, a).start()
        hp_copy(k, a).start()

    first(0)

    @pl.loop(1, LAG)
    def _(k):
        first(k)
        second(k - 1)

    total_squares = ss[a]
    for d in range(1, A):
        q_copy(d).wait_recv()
        total_squares = total_squares + ssr[d - 1]
    inverse = lax.rsqrt(total_squares / D + epsilon)[:, :1]

    @pl.loop(LAG, NF)
    def _(k):
        first(k)
        second(k - 1)
        hidden(k - LAG, inverse)

    second(NF - 1)

    @pl.loop(NF - LAG, NF)
    def _(k):
        hidden(k, inverse)

    @pl.loop(0, NF)
    def _(k):
        hx_copy(k, xpeer).wait_recv()
        hf_copy(k, xpeer).start()

    @pl.loop(0, NF)
    def _(k):
        hp_copy(k, partner).wait_recv()
        hf_copy(k, 2 * (1 - x) + (1 - c)).wait_recv()

    @pl.loop(0, NA)
    def _(n):
        wcopy(wd, wd_v, wd_s, n).wait()
        p = jnp.zeros((Z * RB, T), f32)
        for k in range(NF):
            p = p + jnp.dot(
                hb[k].reshape(Z * RB, T), wd_v[n, k * T:(k + 1) * T, :], preferred_element_type=f32
            )
        p = p.reshape(Z, RB, T)
        fa[...] = p.reshape(fa.shape)
        pd[n] = p.astype(bf)
        od[n] = fa[half, z % 2]
        for d in range(1, Z):
            d_copy(n, d).start()

    for n in range(NA):
        total = res[n, half, z % 2].astype(f32) + od[n]
        for d in range(1, Z):
            d_copy(n, d).wait_recv()
            total = total + rd[n, d - 1].astype(f32)
        out[:, :, n * T:(n + 1) * T] = total.reshape(out.shape[0], STEPS, T).astype(bf)

    for k in range(NA):
        for d in range(1, Z):
            d_copy(k, d).wait_send()

    @pl.when(inside == 0)
    def _():
        for k in range(NA):
            a_copy(k, inner).wait_send()

    @pl.when(inside > 0)
    def _():
        for k in range(NA):
            m_copy(k).wait_send()
            g_copy(k, half).wait_send()
            n_copy(k, half, outer).wait_send()
            f_copy(k, 1 - half, outer).wait_send()

    for d in range(1, A):
        q_copy(d).wait_send()
    for i, (mine, everyone) in enumerate(((q, gq), (kv, gkv))):
        remote(mine, block_of(everyone, a), qx_ss.at[i], qx_rs.at[i], "att", xpeer).wait_send()
        remote(mine, block_of(everyone, a), qp_ss.at[i], qp_rs.at[i], "att", partner).wait_send()
        qf_copy(i, everyone).wait_send()
    for k in range(NA):
        t_copy(k, tx_ss, tx_rs, a, xpeer).wait_send()
        t_copy(k, tp_ss, tp_rs, a, partner).wait_send()
        t_copy(k, tf_ss, tf_rs, xpeer, partner).wait_send()
    for k in range(NF):
        c1_copy(k).wait_send()
        c2_copy(k).wait_send()
        hp_copy(k, a).wait_send()
        hx_copy(k, a).wait_send()
        hf_copy(k, xpeer).wait_send()


def fused(holders, slots, lengths, q, kv, incoming, gain, cache, w_out, w_gate, w_up, w_down):
    Z = lax.axis_size("ffn")
    rows, kdim = slots.shape[0] * STEPS, w_out.shape[0]
    width = w_out.shape[1]
    units = w_gate.shape[1]
    RB, T = rows // Z, TILE
    NA, NF = width // T, units // T
    AB = rows // 4
    S = cache.shape[0]
    bf, f32 = jnp.bfloat16, jnp.float32
    V = pltpu.VMEM
    dma = pltpu.SemaphoreType.DMA
    vm = pl.BlockSpec(memory_space=pltpu.VMEM)
    sm = pl.BlockSpec(memory_space=pltpu.SMEM)
    hbm = pl.BlockSpec(memory_space=pl.ANY)
    scratch = [
        V((rows, rows), bf), V((incoming.shape[0] // 2,) + incoming.shape[1:], bf),
        V((4 * S,) + q.shape[1:], bf), V((4 * S,) + kv.shape[1:], bf),
        V((S * STEPS * (H // KVH), HD), f32), V((kdim // T, 4, AB, T), bf), V((rows, kdim), bf),
        V((NA, kdim, T), bf), V((NF, width, T), bf), V((NF, width, T), bf), V((NA, units, T), bf),
        V((2, 2, RB, T), f32), V((NA, 2, 2, RB, T), bf), V((NA, 2, 2, RB, T), bf), V((NA, 2, RB, T), bf),
        V((NA, 2, RB, T), bf), V((NA, 2, RB, T), f32),
        V((NA, 2, 2, RB, T), bf), V((rows, width), bf), V((4, AB, 128), f32), V((3, AB, 128), f32),
        V((2, 4, AB, T), f32), V((NF, 2, 2, AB, T), bf), V((2, 2, 2, AB, T), f32),
        V((NF, 2, 2, AB, T), bf), V((NF, 2, AB, T), bf), V((NF, 2, AB, T), f32),
        V((NF, 2, AB, T), bf), V((NF, 4, AB, T), bf),
        V((NA, Z, RB, T), bf), V((NA, RB, T), f32), V((NA, Z - 1, RB, T), bf),
        dma((NA,)), dma((NF,)), dma((NF,)), dma((NA,)),
        dma((1,)),
    ] + [dma((NA,)) for _ in range(10)] + [dma((3,)), dma((3,))]
    scratch += [dma((NF,)) for _ in range(10)] + [dma((NA, Z - 1)), dma((NA, Z - 1))]
    scratch += [dma((S,))] + [dma((2,)) for _ in range(6)] + [dma((NA,)) for _ in range(6)]
    return pl.pallas_call(
        functools.partial(layer_kernel, (Z, RB, T, NA, NF)),
        out_shape=jax.ShapeDtypeStruct((RB // STEPS, STEPS, width), bf),
        in_specs=[sm, vm, sm, vm, vm, hbm, vm, hbm, hbm, hbm, hbm, hbm],
        out_specs=vm,
        scratch_shapes=scratch,
        compiler_params=pltpu.CompilerParams(
            collective_id=1, has_side_effects=True, vmem_limit_bytes=67043328
        ),
    )(holders, slots[None], lengths, q, kv, incoming, gain, cache, w_out, w_gate, w_up, w_down)


def fits(queries, cache, w_out, w_gate, slot_of):
    slots = cache.shape[0]
    chunks = w_out.shape[1] // TILE
    return (
        lax.axis_size("att") == 4
        and lax.axis_size("ffn") == 4
        and slots % 16 == 0
        and slots & (slots - 1) == 0
        and slot_of.shape[0] == 4 * slots
        and slot_of.shape[0] * STEPS <= 128
        and cache.shape[2] == TILE
        and w_out.shape == (chunks * TILE, chunks * TILE)
        and w_gate.shape[1] % TILE == 0
        and w_gate.shape[1] // TILE > LAG
        and chunks * (w_gate.shape[1] // CAP) >= slots
    )


def local_fused(
    incoming, queries, new_kv, cache, lengths, slot_of, w_out, norm_gain, w_gate, w_up, w_down
):
    slots = cache.shape[0]
    kv_local, groups = cache.shape[2] // (2 * HD), H // KVH
    q = queries.reshape(slots, STEPS, kv_local, groups, HD).transpose(0, 2, 1, 3, 4)
    kv = new_kv.reshape(slots, STEPS, kv_local, 2, HD).transpose(0, 2, 3, 1, 4)
    requests = jnp.arange(slot_of.shape[0], dtype=jnp.int32)
    own_slots = lax.axis_index("att") * slots + jnp.arange(slots, dtype=jnp.int32)
    held = slot_of[None, :] == own_slots[:, None]
    return fused(
        jnp.sum(jnp.where(held, requests[None, :], 0), 1),
        slot_of,
        lengths,
        q.reshape(slots, -1, HD),
        kv.reshape(slots, -1, HD),
        incoming,
        norm_gain[None],
        cache,
        w_out,
        w_gate,
        w_up,
        w_down,
    )


def local(
    incoming, queries, new_kv, cache, lengths, slot_of, w_out, norm_gain, w_gate, w_up, w_down
):
    if fits(queries, cache, w_out, w_gate, slot_of):
        return local_fused(
            incoming, queries, new_kv, cache, lengths, slot_of,
            w_out, norm_gain, w_gate, w_up, w_down,
        )
    ffn_count = lax.axis_size("ffn")
    att_index = lax.axis_index("att")
    ffn_index = lax.axis_index("ffn")
    request_count = slot_of.shape[0]
    slot_count = cache.shape[0]
    kv_local = cache.shape[2] // (2 * HD)
    groups = H // KVH
    score_scale = HD ** (-0.5)
    gathered_q, gathered_kv = (
        lax.all_gather(queries, "att", axis=0, tiled=True),
        lax.all_gather(new_kv, "att", axis=0, tiled=True),
    )
    holders = (
        jnp.zeros((request_count,), jnp.int32)
        .at[slot_of]
        .set(jnp.arange(request_count, dtype=jnp.int32))
    )
    my_requests = lax.dynamic_slice_in_dim(holders, att_index * slot_count, slot_count)
    query_mine = jnp.take(gathered_q, my_requests, axis=0).reshape(
        slot_count, STEPS, kv_local, groups, HD
    )
    fresh_mine = jnp.take(gathered_kv, my_requests, axis=0).reshape(
        slot_count, STEPS, kv_local, 2, HD
    )
    cache_view = cache.reshape(slot_count, CAP, kv_local, 2, HD)
    fresh_scores = (
        jnp.einsum(
            "rskgd,rtkd->rskgt",
            query_mine,
            fresh_mine[:, :, :, 0],
            preferred_element_type=jnp.float32,
        )
        * score_scale
    )
    causal = jnp.arange(STEPS)[None, :] <= jnp.arange(STEPS)[:, None]
    fresh_scores = jnp.where(causal[None, :, None, None, :], fresh_scores, -jnp.inf)
    kept_scores = (
        jnp.einsum(
            "rskgd,rckd->rskgc",
            query_mine,
            cache_view[:, :, :, 0],
            preferred_element_type=jnp.float32,
        )
        * score_scale
    )
    in_range = jnp.arange(CAP)[None, :] < lengths[:, None]
    kept_scores = jnp.where(in_range[:, None, None, None, :], kept_scores, -jnp.inf)
    top_score = jnp.maximum(jnp.max(kept_scores, -1), jnp.max(fresh_scores, -1))
    kept_exp = jnp.exp(kept_scores - top_score[..., None])
    fresh_exp = jnp.exp(fresh_scores - top_score[..., None])
    denominator = jnp.sum(kept_exp, -1) + jnp.sum(fresh_exp, -1)
    kept_prob = (kept_exp / denominator[..., None]).astype(jnp.bfloat16)
    fresh_prob = (fresh_exp / denominator[..., None]).astype(jnp.bfloat16)
    mixture = jnp.einsum(
        "rskgc,rckd->rskgd", kept_prob, cache_view[:, :, :, 1], preferred_element_type=jnp.float32
    )
    mixture = mixture + jnp.einsum(
        "rskgt,rtkd->rskgd", fresh_prob, fresh_mine[:, :, :, 1], preferred_element_type=jnp.float32
    )
    attended = mixture.astype(jnp.bfloat16).reshape(slot_count, STEPS, kv_local * groups * HD)
    shard_rows = lax.all_gather(attended, "att", axis=0, tiled=True)
    row_count = shard_rows.shape[0]
    flattened = shard_rows.reshape(row_count * STEPS, shard_rows.shape[2])
    heads_slots = jnp.dot(flattened, w_out, preferred_element_type=jnp.float32).reshape(
        row_count, STEPS, w_out.shape[1]
    )
    heads_requests = jnp.take(heads_slots, slot_of, axis=0)
    heads_total = lax.psum(heads_requests, "ffn")
    residual = (incoming.astype(jnp.float32) + heads_total).astype(jnp.bfloat16)
    residual_wide = residual.astype(jnp.float32)
    squares = lax.psum(jnp.sum(residual_wide * residual_wide, -1), "att")
    normed = (residual_wide * lax.rsqrt(squares / D + epsilon)[..., None] * norm_gain).astype(
        jnp.bfloat16
    )
    normed = normed.reshape(request_count * STEPS, normed.shape[2])
    gate_term = jnp.dot(normed, w_gate, preferred_element_type=jnp.float32)
    upward_term = jnp.dot(normed, w_up, preferred_element_type=jnp.float32)
    unit_share = lax.psum_scatter(
        jnp.concatenate([gate_term, upward_term], 1), "att", scatter_dimension=0, tiled=True
    )
    unit_width = w_gate.shape[1]
    hidden_share = (jax.nn.silu(unit_share[:, :unit_width]) * unit_share[:, unit_width:]).astype(
        jnp.bfloat16
    )
    down_part = jnp.dot(
        lax.all_gather(hidden_share, "att", axis=0, tiled=True),
        w_down,
        preferred_element_type=jnp.float32,
    )
    out_share = lax.psum_scatter(down_part, "ffn", scatter_dimension=0, tiled=True)
    row_share = request_count // ffn_count
    own_state = lax.dynamic_slice_in_dim(residual_wide, ffn_index * row_share, row_share, 0)
    return (own_state + out_share.reshape(row_share, STEPS, out_share.shape[1])).astype(
        jnp.bfloat16
    )


def solution(mesh):
    return jax.shard_map(
        local,
        mesh=mesh,
        in_specs=(
            P("parts", None, "att"),
            P(("parts", "att"), None, "ffn"),
            P(("parts", "att"), None, "ffn"),
            P(("parts", "att"), None, "ffn"),
            P(("parts", "att")),
            P("parts"),
            P("ffn", "att"),
            P("att"),
            P("att", "ffn"),
            P("att", "ffn"),
            P("ffn", "att"),
        ),
        out_specs=P(("parts", "ffn"), None, "att"),
        check_vma=False,
    )
```

```python
import functools

import jax
import jax.numpy as jnp
from jax import lax
from jax.experimental import pallas as pl
from jax.experimental.pallas import tpu as pltpu
from jax.sharding import PartitionSpec as P

D = 8192
H = 64
KVH = 8
HD = 128
STEPS = 2
CAP = 640


epsilon = 1e-05
TILE = 512
MESH = pl.DeviceIdType.MESH


def layer_kernel(
    cfg, holders, slots_row, lengths, q, kv, incoming, gain, cache, wo, wg, wu, wd, out,
    place, kept_in, gq, gkv, of, tb, attended,
    wo_v, wg_v, wu_v, wd_v,
    fa, pa, ra, sm, rm, om, res, h, ss, ssr,
    fg, s1, o1, r1, s2, o2, r2, hb,
    pd, od, rd,
    wo_s, wg_s, wu_s, wd_s,
    in_s, a_ss, a_rs, m_ss, m_rs, g_ss, g_rs, n_ss, n_rs, f_ss, f_rs, q_ss, q_rs,
    c1_ss, c1_rs, c2_ss, c2_rs,
    hp_ss, hp_rs, hx_ss, hx_rs, hf_ss, hf_rs,
    d_ss, d_rs,
    cache_s, qp_ss, qp_rs, qx_ss, qx_rs, qf_ss, qf_rs,
    tp_ss, tp_rs, tx_ss, tx_rs, tf_ss, tf_rs,
):
    Z, RB, T, NA, NF = cfg
    S = cache.shape[0]
    kv_local = cache.shape[2] // (2 * HD)
    groups = H // KVH
    QR = STEPS * groups
    per = wd_v.shape[1] // CAP
    A = 4
    z = lax.axis_index("ffn")
    a = lax.axis_index("att")
    x, c = a // 2, a % 2
    partner = 2 * x + (1 - c)
    xpeer = 2 * (1 - x) + c
    bf, f32 = jnp.bfloat16, jnp.float32

    def wcopy(src, dst, sem, k):
        return pltpu.make_async_copy(
            src.at[:, pl.ds(pl.multiple_of(k * T, T), T)], dst.at[k], sem.at[k]
        )

    def kept_rows(i):
        return pl.ds(pl.multiple_of((i % per) * CAP, CAP), CAP)

    def cache_copy(i):
        return pltpu.make_async_copy(cache.at[i], wd_v.at[i // per, kept_rows(i)], cache_s.at[i])

    @pl.loop(0, S)
    def _(i):
        cache_copy(i).start()

    half = z // 2
    in_copy = pltpu.make_async_copy(
        incoming.at[pl.ds(half * kept_in.shape[0], kept_in.shape[0])], kept_in, in_s.at[0]
    )
    in_copy.start()
    for k in range(NA):
        wcopy(wo, wo_v, wo_s, k).start()
    for k in range(NF):
        wcopy(wg, wg_v, wg_s, k).start()
        wcopy(wu, wu_v, wu_s, k).start()

    barrier = pltpu.get_barrier_semaphore()
    for d in range(1, Z):
        pl.semaphore_signal(barrier, 1, device_id={"ffn": (z + d) % Z}, device_id_type=MESH)
    for d in range(1, A):
        pl.semaphore_signal(barrier, 1, device_id={"att": (a + d) % A}, device_id_type=MESH)
    pl.semaphore_wait(barrier, Z - 1 + A - 1)

    def remote(src, dst, ss_, rs_, axis, peer):
        return pltpu.make_async_remote_copy(
            src_ref=src, dst_ref=dst, send_sem=ss_, recv_sem=rs_,
            device_id={axis: peer}, device_id_type=MESH,
        )

    inside = z * (Z - 1 - z)
    inner = 1 + half
    outer = 3 * (z - 1)
    other = 3 - z

    def half_of(ref, k, which):
        return ref.at[k, which]

    def a_copy(k, peer):
        return remote(pa.at[k], ra.at[k], a_ss.at[k], a_rs.at[k], "ffn", peer)

    def m_copy(k):
        return remote(sm.at[k], rm.at[k], m_ss.at[k], m_rs.at[k], "ffn", other)

    def g_copy(k, which):
        block = half_of(res, k, which)
        return remote(block, block, g_ss.at[k], g_rs.at[k], "ffn", other)

    def n_copy(k, which, peer):
        block = half_of(res, k, which)
        return remote(block, block, n_ss.at[k], n_rs.at[k], "ffn", peer)

    def f_copy(k, which, peer):
        block = half_of(res, k, which)
        return remote(block, block, f_ss.at[k], f_rs.at[k], "ffn", peer)

    def q_copy(d):
        peer = (a + d) % A
        return remote(ss.at[peer], ssr.at[d - 1], q_ss.at[d - 1], q_rs.at[d - 1], "att", peer)

    def c1_copy(k):
        return remote(s1.at[k], r1.at[k], c1_ss.at[k], c1_rs.at[k], "att", partner)

    def c2_copy(k):
        return remote(s2.at[k], r2.at[k], c2_ss.at[k], c2_rs.at[k], "att", xpeer)

    def hp_copy(k, block):
        return remote(hb.at[k, block], hb.at[k, block], hp_ss.at[k], hp_rs.at[k], "att", partner)

    def hx_copy(k, block):
        return remote(hb.at[k, block], hb.at[k, block], hx_ss.at[k], hx_rs.at[k], "att", xpeer)

    def hf_copy(k, block):
        return remote(hb.at[k, block], hb.at[k, block], hf_ss.at[k], hf_rs.at[k], "att", partner)

    def d_copy(k, d):
        peer = (z + d) % Z
        return remote(pd.at[k, peer], rd.at[k, d - 1], d_ss.at[k, d - 1], d_rs.at[k, d - 1], "ffn", peer)

    def block_of(ref, owner):
        return ref.at[pl.ds(owner * S, S)]

    for i, (mine, everyone) in enumerate(((q, gq), (kv, gkv))):
        remote(mine, block_of(everyone, a), qx_ss.at[i], qx_rs.at[i], "att", xpeer).start()
        remote(mine, block_of(everyone, a), qp_ss.at[i], qp_rs.at[i], "att", partner).start()
        everyone[pl.ds(a * S, S)] = mine[...]

    def qf_copy(i, everyone):
        block = block_of(everyone, xpeer)
        return remote(block, block, qf_ss.at[i], qf_rs.at[i], "att", partner)

    R = slots_row.shape[1]

    shift = S.bit_length() - 1
    spread_row = lax.broadcasted_iota(jnp.int32, (R, R * STEPS), 0) * STEPS
    spread_col = lax.broadcasted_iota(jnp.int32, (R, R * STEPS), 1)
    spread = (spread_col >= spread_row) & (spread_col < spread_row + STEPS)
    slot_at = jnp.dot(
        jnp.broadcast_to(slots_row[...].astype(f32), (8, R)).astype(bf),
        jnp.where(spread, 1.0, 0.0).astype(bf),
        preferred_element_type=f32,
    )[:1]
    row = lax.broadcasted_iota(jnp.int32, (R * STEPS, R * STEPS), 0)
    col = lax.broadcasted_iota(jnp.int32, (R * STEPS, R * STEPS), 1)
    row_slot = ((row >> (shift + 1)) << shift) + (row & (S - 1))
    row_step = (row >> shift) & (STEPS - 1)
    chosen = (row_slot.astype(f32) == slot_at) & (row_step == (col & (STEPS - 1)))
    place[...] = jnp.where(chosen, 1.0, 0.0).astype(bf)

    far = 2 * (1 - x) + (1 - c)
    for i, (mine, everyone) in enumerate(((q, gq), (kv, gkv))):
        remote(mine, block_of(everyone, xpeer), qx_ss.at[i], qx_rs.at[i], "att", xpeer).wait_recv()
        qf_copy(i, everyone).start()
    for i, (mine, everyone) in enumerate(((q, gq), (kv, gkv))):
        remote(mine, block_of(everyone, partner), qp_ss.at[i], qp_rs.at[i], "att", partner).wait_recv()
        block = block_of(everyone, far)
        remote(block, block, qf_ss.at[i], qf_rs.at[i], "att", partner).wait_recv()

    def attend(i, g):
        holder, length = holders[i], lengths[i]
        rows = gq[holder][g * QR:(g + 1) * QR]
        fresh = gkv[holder].astype(f32)
        kept = kept_rows(i)
        keys = wd_v[i // per, kept, g * 2 * HD:(g * 2 + 1) * HD]
        values = wd_v[i // per, kept, (g * 2 + 1) * HD:(g * 2 + 2) * HD]
        scale = HD ** (-0.5)
        scores = lax.dot_general(
            rows, keys, (((1,), (1,)), ((), ())), preferred_element_type=f32
        ) * scale
        column = lax.broadcasted_iota(jnp.int32, scores.shape, 1)
        scores = jnp.where(column < length, scores, -jnp.inf)
        wide = rows.astype(f32)
        step = lax.broadcasted_iota(jnp.int32, (QR, 1), 0) // groups
        new_scores = []
        for t in range(STEPS):
            at = g * 2 * STEPS + t
            score = jnp.sum(wide * fresh[at:at + 1], -1, keepdims=True) * scale
            new_scores.append(jnp.where(step >= t, score, -jnp.inf))
        top = jnp.max(scores, -1, keepdims=True)
        for score in new_scores:
            top = jnp.maximum(top, score)
        weights = jnp.exp(scores - top)
        total = jnp.sum(weights, -1, keepdims=True)
        new_weights = [jnp.exp(score - top) for score in new_scores]
        for weight in new_weights:
            total = total + weight
        mixed = jnp.dot((weights / total).astype(bf), values, preferred_element_type=f32)
        for t in range(STEPS):
            at = g * 2 * STEPS + STEPS + t
            mixed = mixed + (new_weights[t] / total).astype(bf).astype(f32) * fresh[at:at + 1]
        of[pl.ds(pl.multiple_of(i * QR, QR), QR), :] = mixed

    def t_copy(k, ss_, rs_, block, peer):
        return remote(tb.at[k, block], tb.at[k, block], ss_.at[k], rs_.at[k], "att", peer)

    heads = T // HD
    chunks = groups // heads
    for g in range(kv_local):
        @pl.loop(0, S // 8)
        def _(j):
            for n in range(8):
                if g == 0:
                    cache_copy(j * 8 + n).wait()
            for n in range(8):
                attend(j * 8 + n, g)

        for k in range(chunks):
            for t in range(STEPS):
                for n in range(heads):
                    row = t * groups + k * heads + n
                    tb[g * chunks + k, a, t * S:(t + 1) * S, n * HD:(n + 1) * HD] = of[
                        pl.ds(row, S, stride=QR), :
                    ].astype(bf)
            t_copy(g * chunks + k, tx_ss, tx_rs, a, xpeer).start()
            t_copy(g * chunks + k, tp_ss, tp_rs, a, partner).start()

    for k in range(NA):
        wcopy(wd, wd_v, wd_s, k).start()
    for k in range(NA):
        t_copy(k, tx_ss, tx_rs, xpeer, xpeer).wait_recv()
        t_copy(k, tf_ss, tf_rs, xpeer, partner).start()
    for k in range(NA):
        t_copy(k, tp_ss, tp_rs, partner, partner).wait_recv()
        t_copy(k, tf_ss, tf_rs, far, partner).wait_recv()
        attended[:, k * T:(k + 1) * T] = lax.dot_general(
            place[...], tb[k].reshape(Z * RB, T), (((0,), (0,)), ((), ())),
            preferred_element_type=f32,
        ).astype(bf)

    in_copy.wait()

    def own_half(k):
        m_copy(k).wait_recv()
        kept = kept_in[:, :, k * T:(k + 1) * T].astype(f32).reshape(2, RB, T)
        res[k, half] = (kept + om[k] + rm[k].astype(f32)).astype(bf)
        g_copy(k, half).start()
        n_copy(k, half, outer).start()

    def pass_on(k):
        g_copy(k, 1 - half).wait_recv()
        f_copy(k, 1 - half, outer).start()

    for k in range(NA):
        wcopy(wo, wo_v, wo_s, k).wait()
        fa[...] = jnp.dot(attended[...], wo_v[k], preferred_element_type=f32).reshape(fa.shape)

        @pl.when(inside == 0)
        def _():
            pa[k] = fa[...].astype(bf)
            a_copy(k, inner).start()

        @pl.when(inside > 0)
        def _():
            a_copy(k, outer).wait_recv()
            theirs = 1 - half
            sm[k] = (fa[theirs] + ra[k, theirs].astype(f32)).astype(bf)
            m_copy(k).start()
            om[k] = fa[half] + ra[k, half].astype(f32)
            if k > 0:
                own_half(k - 1)
            if k > 1:
                pass_on(k - 2)

    @pl.when(inside > 0)
    def _():
        own_half(NA - 1)
        for k in range(max(NA - 2, 0), NA):
            pass_on(k)

    squares = jnp.zeros((Z, RB, 1), f32)
    for k in range(NA):
        @pl.when(inside == 0)
        def _():
            n_copy(k, half, inner).wait_recv()
            f_copy(k, 1 - half, inner).wait_recv()

        wide = res[k].astype(f32).reshape(Z, RB, T)
        squares = squares + jnp.sum(wide * wide, -1, keepdims=True)
        h[:, k * T:(k + 1) * T] = (
            (wide * gain[:, k * T:(k + 1) * T]).astype(bf).reshape(Z * RB, T)
        )
    ss[...] = jnp.broadcast_to(squares.reshape(A, ss.shape[1], 1), ss.shape)
    for d in range(1, A):
        q_copy(d).start()

    def first(k):
        wcopy(wg, wg_v, wg_s, k).wait()
        wcopy(wu, wu_v, wu_s, k).wait()
        for i, w in enumerate((wg_v, wu_v)):
            p = jnp.dot(h[...], w[k], preferred_element_type=f32)
            fg[i] = p.reshape(fg.shape[1:])
            for xx in range(2):
                s1[k, i, xx] = fg[i, 2 * xx + (1 - c)].astype(bf)
                o1[k % 2, i, xx] = fg[i, 2 * xx + c]
        c1_copy(k).start()

    def second(k):
        c1_copy(k).wait_recv()
        for i in range(2):
            s2[k, i] = (o1[k % 2, i, 1 - x] + r1[k, i, 1 - x].astype(f32)).astype(bf)
            o2[k, i] = o1[k % 2, i, x] + r1[k, i, x].astype(f32)
        c2_copy(k).start()

    first(0)

    @pl.loop(1, NF)
    def _(k):
        first(k)
        second(k - 1)

    second(NF - 1)

    total_squares = ss[a]
    for d in range(1, A):
        q_copy(d).wait_recv()
        total_squares = total_squares + ssr[d - 1]
    inverse = lax.rsqrt(total_squares / D + epsilon)[:, :1]

    @pl.loop(0, NF)
    def _(k):
        c2_copy(k).wait_recv()
        gate = (o2[k, 0] + r2[k, 0].astype(f32)) * inverse
        up = (o2[k, 1] + r2[k, 1].astype(f32)) * inverse
        hb[k, a] = (gate / (1.0 + jnp.exp(-gate)) * up).astype(bf)
        hx_copy(k, a).start()
        hp_copy(k, a).start()

    @pl.loop(0, NF)
    def _(k):
        hx_copy(k, xpeer).wait_recv()
        hf_copy(k, xpeer).start()

    @pl.loop(0, NF)
    def _(k):
        hp_copy(k, partner).wait_recv()
        hf_copy(k, 2 * (1 - x) + (1 - c)).wait_recv()

    @pl.loop(0, NA)
    def _(n):
        wcopy(wd, wd_v, wd_s, n).wait()
        p = jnp.zeros((Z * RB, T), f32)
        for k in range(NF):
            p = p + jnp.dot(
                hb[k].reshape(Z * RB, T), wd_v[n, k * T:(k + 1) * T, :], preferred_element_type=f32
            )
        p = p.reshape(Z, RB, T)
        fa[...] = p.reshape(fa.shape)
        pd[n] = p.astype(bf)
        od[n] = fa[half, z % 2]
        for d in range(1, Z):
            d_copy(n, d).start()

    for n in range(NA):
        total = res[n, half, z % 2].astype(f32) + od[n]
        for d in range(1, Z):
            d_copy(n, d).wait_recv()
            total = total + rd[n, d - 1].astype(f32)
        out[:, :, n * T:(n + 1) * T] = total.reshape(out.shape[0], STEPS, T).astype(bf)

    for k in range(NA):
        for d in range(1, Z):
            d_copy(k, d).wait_send()

    @pl.when(inside == 0)
    def _():
        for k in range(NA):
            a_copy(k, inner).wait_send()

    @pl.when(inside > 0)
    def _():
        for k in range(NA):
            m_copy(k).wait_send()
            g_copy(k, half).wait_send()
            n_copy(k, half, outer).wait_send()
            f_copy(k, 1 - half, outer).wait_send()

    for d in range(1, A):
        q_copy(d).wait_send()
    for i, (mine, everyone) in enumerate(((q, gq), (kv, gkv))):
        remote(mine, block_of(everyone, a), qx_ss.at[i], qx_rs.at[i], "att", xpeer).wait_send()
        remote(mine, block_of(everyone, a), qp_ss.at[i], qp_rs.at[i], "att", partner).wait_send()
        qf_copy(i, everyone).wait_send()
    for k in range(NA):
        t_copy(k, tx_ss, tx_rs, a, xpeer).wait_send()
        t_copy(k, tp_ss, tp_rs, a, partner).wait_send()
        t_copy(k, tf_ss, tf_rs, xpeer, partner).wait_send()
    for k in range(NF):
        c1_copy(k).wait_send()
        c2_copy(k).wait_send()
        hp_copy(k, a).wait_send()
        hx_copy(k, a).wait_send()
        hf_copy(k, xpeer).wait_send()


def fused(holders, slots, lengths, q, kv, incoming, gain, cache, w_out, w_gate, w_up, w_down):
    Z = lax.axis_size("ffn")
    rows, kdim = slots.shape[0] * STEPS, w_out.shape[0]
    width = w_out.shape[1]
    units = w_gate.shape[1]
    RB, T = rows // Z, TILE
    NA, NF = width // T, units // T
    AB = rows // 4
    S = cache.shape[0]
    bf, f32 = jnp.bfloat16, jnp.float32
    V = pltpu.VMEM
    dma = pltpu.SemaphoreType.DMA
    vm = pl.BlockSpec(memory_space=pltpu.VMEM)
    sm = pl.BlockSpec(memory_space=pltpu.SMEM)
    hbm = pl.BlockSpec(memory_space=pl.ANY)
    scratch = [
        V((rows, rows), bf), V((incoming.shape[0] // 2,) + incoming.shape[1:], bf),
        V((4 * S,) + q.shape[1:], bf), V((4 * S,) + kv.shape[1:], bf),
        V((S * STEPS * (H // KVH), HD), f32), V((kdim // T, 4, AB, T), bf), V((rows, kdim), bf),
        V((NA, kdim, T), bf), V((NF, width, T), bf), V((NF, width, T), bf), V((NA, units, T), bf),
        V((2, 2, RB, T), f32), V((NA, 2, 2, RB, T), bf), V((NA, 2, 2, RB, T), bf), V((NA, 2, RB, T), bf),
        V((NA, 2, RB, T), bf), V((NA, 2, RB, T), f32),
        V((NA, 2, 2, RB, T), bf), V((rows, width), bf), V((4, AB, 128), f32), V((3, AB, 128), f32),
        V((2, 4, AB, T), f32), V((NF, 2, 2, AB, T), bf), V((2, 2, 2, AB, T), f32),
        V((NF, 2, 2, AB, T), bf), V((NF, 2, AB, T), bf), V((NF, 2, AB, T), f32),
        V((NF, 2, AB, T), bf), V((NF, 4, AB, T), bf),
        V((NA, Z, RB, T), bf), V((NA, RB, T), f32), V((NA, Z - 1, RB, T), bf),
        dma((NA,)), dma((NF,)), dma((NF,)), dma((NA,)),
        dma((1,)),
    ] + [dma((NA,)) for _ in range(10)] + [dma((3,)), dma((3,))]
    scratch += [dma((NF,)) for _ in range(10)] + [dma((NA, Z - 1)), dma((NA, Z - 1))]
    scratch += [dma((S,))] + [dma((2,)) for _ in range(6)] + [dma((NA,)) for _ in range(6)]
    return pl.pallas_call(
        functools.partial(layer_kernel, (Z, RB, T, NA, NF)),
        out_shape=jax.ShapeDtypeStruct((RB // STEPS, STEPS, width), bf),
        in_specs=[sm, vm, sm, vm, vm, hbm, vm, hbm, hbm, hbm, hbm, hbm],
        out_specs=vm,
        scratch_shapes=scratch,
        compiler_params=pltpu.CompilerParams(
            collective_id=1, has_side_effects=True, vmem_limit_bytes=67043328
        ),
    )(holders, slots[None], lengths, q, kv, incoming, gain, cache, w_out, w_gate, w_up, w_down)


def fits(queries, cache, w_out, w_gate, slot_of):
    slots = cache.shape[0]
    chunks = w_out.shape[1] // TILE
    return (
        lax.axis_size("att") == 4
        and lax.axis_size("ffn") == 4
        and slots % 16 == 0
        and slots & (slots - 1) == 0
        and slot_of.shape[0] == 4 * slots
        and slot_of.shape[0] * STEPS <= 128
        and cache.shape[2] == TILE
        and w_out.shape == (chunks * TILE, chunks * TILE)
        and w_gate.shape[1] % TILE == 0
        and chunks * (w_gate.shape[1] // CAP) >= slots
    )


def local_fused(
    incoming, queries, new_kv, cache, lengths, slot_of, w_out, norm_gain, w_gate, w_up, w_down
):
    slots = cache.shape[0]
    kv_local, groups = cache.shape[2] // (2 * HD), H // KVH
    q = queries.reshape(slots, STEPS, kv_local, groups, HD).transpose(0, 2, 1, 3, 4)
    kv = new_kv.reshape(slots, STEPS, kv_local, 2, HD).transpose(0, 2, 3, 1, 4)
    requests = jnp.arange(slot_of.shape[0], dtype=jnp.int32)
    own_slots = lax.axis_index("att") * slots + jnp.arange(slots, dtype=jnp.int32)
    held = slot_of[None, :] == own_slots[:, None]
    return fused(
        jnp.sum(jnp.where(held, requests[None, :], 0), 1),
        slot_of,
        lengths,
        q.reshape(slots, -1, HD),
        kv.reshape(slots, -1, HD),
        incoming,
        norm_gain[None],
        cache,
        w_out,
        w_gate,
        w_up,
        w_down,
    )


def local(
    incoming, queries, new_kv, cache, lengths, slot_of, w_out, norm_gain, w_gate, w_up, w_down
):
    if fits(queries, cache, w_out, w_gate, slot_of):
        return local_fused(
            incoming, queries, new_kv, cache, lengths, slot_of,
            w_out, norm_gain, w_gate, w_up, w_down,
        )
    ffn_count = lax.axis_size("ffn")
    att_index = lax.axis_index("att")
    ffn_index = lax.axis_index("ffn")
    request_count = slot_of.shape[0]
    slot_count = cache.shape[0]
    kv_local = cache.shape[2] // (2 * HD)
    groups = H // KVH
    score_scale = HD ** (-0.5)
    gathered_q, gathered_kv = (
        lax.all_gather(queries, "att", axis=0, tiled=True),
        lax.all_gather(new_kv, "att", axis=0, tiled=True),
    )
    holders = (
        jnp.zeros((request_count,), jnp.int32)
        .at[slot_of]
        .set(jnp.arange(request_count, dtype=jnp.int32))
    )
    my_requests = lax.dynamic_slice_in_dim(holders, att_index * slot_count, slot_count)
    query_mine = jnp.take(gathered_q, my_requests, axis=0).reshape(
        slot_count, STEPS, kv_local, groups, HD
    )
    fresh_mine = jnp.take(gathered_kv, my_requests, axis=0).reshape(
        slot_count, STEPS, kv_local, 2, HD
    )
    cache_view = cache.reshape(slot_count, CAP, kv_local, 2, HD)
    fresh_scores = (
        jnp.einsum(
            "rskgd,rtkd->rskgt",
            query_mine,
            fresh_mine[:, :, :, 0],
            preferred_element_type=jnp.float32,
        )
        * score_scale
    )
    causal = jnp.arange(STEPS)[None, :] <= jnp.arange(STEPS)[:, None]
    fresh_scores = jnp.where(causal[None, :, None, None, :], fresh_scores, -jnp.inf)
    kept_scores = (
        jnp.einsum(
            "rskgd,rckd->rskgc",
            query_mine,
            cache_view[:, :, :, 0],
            preferred_element_type=jnp.float32,
        )
        * score_scale
    )
    in_range = jnp.arange(CAP)[None, :] < lengths[:, None]
    kept_scores = jnp.where(in_range[:, None, None, None, :], kept_scores, -jnp.inf)
    top_score = jnp.maximum(jnp.max(kept_scores, -1), jnp.max(fresh_scores, -1))
    kept_exp = jnp.exp(kept_scores - top_score[..., None])
    fresh_exp = jnp.exp(fresh_scores - top_score[..., None])
    denominator = jnp.sum(kept_exp, -1) + jnp.sum(fresh_exp, -1)
    kept_prob = (kept_exp / denominator[..., None]).astype(jnp.bfloat16)
    fresh_prob = (fresh_exp / denominator[..., None]).astype(jnp.bfloat16)
    mixture = jnp.einsum(
        "rskgc,rckd->rskgd", kept_prob, cache_view[:, :, :, 1], preferred_element_type=jnp.float32
    )
    mixture = mixture + jnp.einsum(
        "rskgt,rtkd->rskgd", fresh_prob, fresh_mine[:, :, :, 1], preferred_element_type=jnp.float32
    )
    attended = mixture.astype(jnp.bfloat16).reshape(slot_count, STEPS, kv_local * groups * HD)
    shard_rows = lax.all_gather(attended, "att", axis=0, tiled=True)
    row_count = shard_rows.shape[0]
    flattened = shard_rows.reshape(row_count * STEPS, shard_rows.shape[2])
    heads_slots = jnp.dot(flattened, w_out, preferred_element_type=jnp.float32).reshape(
        row_count, STEPS, w_out.shape[1]
    )
    heads_requests = jnp.take(heads_slots, slot_of, axis=0)
    heads_total = lax.psum(heads_requests, "ffn")
    residual = (incoming.astype(jnp.float32) + heads_total).astype(jnp.bfloat16)
    residual_wide = residual.astype(jnp.float32)
    squares = lax.psum(jnp.sum(residual_wide * residual_wide, -1), "att")
    normed = (residual_wide * lax.rsqrt(squares / D + epsilon)[..., None] * norm_gain).astype(
        jnp.bfloat16
    )
    normed = normed.reshape(request_count * STEPS, normed.shape[2])
    gate_term = jnp.dot(normed, w_gate, preferred_element_type=jnp.float32)
    upward_term = jnp.dot(normed, w_up, preferred_element_type=jnp.float32)
    unit_share = lax.psum_scatter(
        jnp.concatenate([gate_term, upward_term], 1), "att", scatter_dimension=0, tiled=True
    )
    unit_width = w_gate.shape[1]
    hidden_share = (jax.nn.silu(unit_share[:, :unit_width]) * unit_share[:, unit_width:]).astype(
        jnp.bfloat16
    )
    down_part = jnp.dot(
        lax.all_gather(hidden_share, "att", axis=0, tiled=True),
        w_down,
        preferred_element_type=jnp.float32,
    )
    out_share = lax.psum_scatter(down_part, "ffn", scatter_dimension=0, tiled=True)
    row_share = request_count // ffn_count
    own_state = lax.dynamic_slice_in_dim(residual_wide, ffn_index * row_share, row_share, 0)
    return (own_state + out_share.reshape(row_share, STEPS, out_share.shape[1])).astype(
        jnp.bfloat16
    )


def solution(mesh):
    return jax.shard_map(
        local,
        mesh=mesh,
        in_specs=(
            P("parts", None, "att"),
            P(("parts", "att"), None, "ffn"),
            P(("parts", "att"), None, "ffn"),
            P(("parts", "att"), None, "ffn"),
            P(("parts", "att")),
            P("parts"),
            P("ffn", "att"),
            P("att"),
            P("att", "ffn"),
            P("att", "ffn"),
            P("ffn", "att"),
        ),
        out_specs=P(("parts", "ffn"), None, "att"),
        check_vma=False,
    )
```
